32 devices in a mesh: cuts: 8 (over z, x), space: 4 (over y, core).
Axes of the slice: x: 2, y: 2, z: 4, core: 2. Of those that a mesh axis runs over, the one named last changes fastest.
Arguments:
- start_old: float32 [8, 16, 2, 2048], P('cuts', None, None, 'space'), may hold values from -3 to 3
- scales: float32 [8, 2, 2048], P('cuts', None, 'space'), may hold values from 0.92 to 1
- propagator: bfloat16 [2, 2048, 2, 2048], P(None, 'space'), may hold values from -1.2 to 1.2
- pipe_of_cell: int32 [8192], P('space'), may hold values from 0 to 127
- friction: float32 [128], replicated, may hold values from 0.02 to 0.2
Outputs:
- end_new: float32 [8, 16, 2, 2048], P('cuts', None, None, 'space')
The draws below stay inside these ranges and needn't reach their ends.
All inputs are finite; a program needn't handle non-finite values.
Results may differ from the reference program's by a relative error of at most 0.0048.
Values may be sent and summed in bfloat16 or wider, within the bound.
A program may use at most 64 MiB of HBM per device.

```python
import math
import jax
import jax.numpy as jnp
from jax import lax

NCC = 2048
REFINE = 4
STEPS = 16
NPIPE = 128
SCEN = 16
SLICES = 8
NCELL = 8192


def draw_propagator(key, part):
    matrix_order = 2 * NCC
    noise_share = 0.5
    norm_fix = 1.0 / math.sqrt(1.0 + noise_share * noise_share)
    key_perm = jax.random.fold_in(key, 11)
    key_sign = jax.random.fold_in(key, 23)
    key_noise = jax.random.fold_in(key, 37)
    target = jax.random.permutation(key_perm, matrix_order).astype(jnp.int32)
    row_signs = (2 * jax.random.randint(key_sign, (matrix_order,), 0, 2) - 1).astype(jnp.float32)
    columns = lax.broadcasted_iota(jnp.int32, (matrix_order, matrix_order), 1)
    signed_perm = jnp.where(columns == target[:, None], row_signs[:, None], 0.0).astype(jnp.float32)
    perturbation = jnp.clip(jax.random.normal(key_noise, (matrix_order, matrix_order), jnp.float32), -4.0, 4.0)
    matrix = norm_fix * (signed_perm + noise_share / math.sqrt(matrix_order) * perturbation)
    return matrix.reshape(2, NCC, 2, NCC).astype(jnp.bfloat16)


def touch_ends(array, rng, least, top_value):
    shape = array.shape
    index_at = [jax.random.randint(jax.random.fold_in(rng, axis), (), 0, shape[axis]) for axis in range(len(shape))]
    array = array.at[tuple(index_at)].set(least)
    longest = shape.index(max(shape))
    index_at[longest] = (index_at[longest] + 1) % shape[longest]
    return array.at[tuple(index_at)].set(top_value)


def block_scale(key, dims, pieces, least, high):
    def one(axis_at, shards_of):
        draws = jax.random.uniform(jax.random.fold_in(jax.random.fold_in(key, 6), axis_at), (shards_of,), jnp.float32, least / len(pieces), high / len(pieces))
        return jnp.repeat(jnp.exp(draws), dims[axis_at] // shards_of).reshape((-1,) + (1,) * (len(dims) - axis_at - 1))

    loudness = one(*pieces[0])
    for cut in pieces[1:]:
        loudness = loudness * one(*cut)
    return loudness


def bell_draw(rng, dims, deviation, bound, pieces=(), dtype=jnp.bfloat16):
    drawn = jax.random.normal(rng, dims, jnp.float32) * deviation
    if len(pieces) > 0:
        drawn = block_scale(rng, dims, pieces, -0.22, 0.18) * drawn
    return jnp.clip(drawn, min=-bound, max=bound).astype(dtype)


def setup_inputs(seed: int = 0) -> dict:
    keys = jax.random.split(jax.random.key(seed), 6)
    start_old = bell_draw(keys[0], (SLICES, SCEN, 2, NCC), 0.5, 3.0, ((0, 8), (3, 4)), jnp.float32)
    scales = jnp.clip(jnp.exp(math.log(1.0) - 0.08338159 * jax.random.uniform(keys[1], (SLICES, 2, NCC), jnp.float32) ** block_scale(keys[1], (SLICES, 2, NCC), ((0, 8), (2, 4)), -0.2, 0.2)), 0.92, 1.0)
    propagator = draw_propagator(jax.random.fold_in(keys[5], 71), 0)
    pipe_of_cell = touch_ends(jax.random.randint(keys[3], (NCELL,), 0, NPIPE), jax.random.fold_in(keys[3], 1), 0, NPIPE - 1).astype(jnp.int32)
    friction = jnp.clip(jnp.exp(jax.random.uniform(keys[4], (NPIPE,), jnp.float32, math.log(0.02), math.log(0.2))), 0.02, 0.2)
    return {"start_old": start_old, "scales": scales, "propagator": propagator, "pipe_of_cell": pipe_of_cell, "friction": friction}


def moc_step(head, flow, rate):
    hleft, hright = head[..., :-2], head[..., 2:]
    qleft, qright = flow[..., :-2], flow[..., 2:]
    plus = hleft + qleft - rate * qleft * jnp.abs(qleft)
    minus = hright - qright + rate * qright * jnp.abs(qright)
    return 0.5 * (plus + minus), 0.5 * (plus - minus)


def reference(start_old, scales, propagator, pipe_of_cell, friction):
    rate = friction[pipe_of_cell]
    field = jnp.repeat(start_old, REFINE, axis=-1)
    head, flow = field[:, :, 0, :], field[:, :, 1, :]
    widths = ((0, 0), (0, 0), (1, 1))
    for step in range(STEPS):
        head, flow = moc_step(jnp.pad(head, widths), jnp.pad(flow, widths), rate)
    fine_field = jnp.stack([head, flow], axis=2)
    fine_coarse = jnp.mean(fine_field.reshape(SLICES, SCEN, 2, NCC, REFINE), axis=-1)
    matrix = propagator.astype(jnp.float32)
    old_scaled = (scales[:, None] * start_old).astype(jnp.bfloat16)
    old_image = jnp.einsum("fiqj,nbqj->nbfi", matrix, old_scaled.astype(jnp.float32))
    delta = fine_coarse - old_image

    def advance(start, inputs):
        scale_now, delta_now = inputs
        scaled = (scale_now[None] * start).astype(jnp.bfloat16)
        ending = jnp.einsum("fiqj,bqj->bfi", matrix, scaled.astype(jnp.float32)) + delta_now
        return ending, ending

    final, end_new = lax.scan(advance, start_old[0], (scales, delta))
    return end_new
```

```python
import functools
import math

import jax
import jax.numpy as jnp
from jax import lax
from jax.experimental import pallas as pl
from jax.experimental.pallas import tpu as pltpu
from jax.sharding import PartitionSpec as P

REFINE = 4
STEPS = 16
LANES = 128
HALF = LANES // 2
ROWS = 128
EARLY = 3
MESH = pl.DeviceIdType.MESH


def kernel(
    cuts, space, groups, x_hbm, scl_hbm, prop_hbm, pipe_hbm, fric_hbm, out_ref,
    x_in, scl_in, pipe_in, fric_in, raw, weight, rates, edge_out, edge_in, first_x, first_scl,
    own, pack, dl, start, xg, last_out, last_in, res_out, res_in,
    in_sem, raw_sem, ready, edge_send, edge_recv, first_send, first_recv, dl_send, dl_recv,
    start_send, xg_send, xg_recv, last_send, last_recv, res_send, res_recv,
):
    c = lax.axis_index("cuts")
    s = lax.axis_index("space")
    scen, cl = x_in.shape[1], x_in.shape[3]
    width = 2 * cl
    nv = cl // LANES
    ext = cl + LANES
    share = scen // groups
    fine = REFINE * LANES
    last = cuts - 1
    chunks = raw.shape[0] // ROWS
    member = c < groups

    inputs = [
        pltpu.make_async_copy(pipe_hbm, pipe_in, in_sem.at[0]),
        pltpu.make_async_copy(fric_hbm, fric_in, in_sem.at[1]),
        pltpu.make_async_copy(x_hbm, x_in, in_sem.at[2]),
        pltpu.make_async_copy(scl_hbm, scl_in, in_sem.at[3]),
    ]
    for copy in inputs:
        copy.start()

    def raw_copy(k):
        at = pl.ds(pl.multiple_of(k * ROWS, ROWS), ROWS)
        return pltpu.make_async_copy(prop_hbm.at[at], raw.at[at], raw_sem.at[k])

    for k in range(chunks):
        raw_copy(k).start()

    barrier = pltpu.get_barrier_semaphore()
    for d in range(1, space):
        pl.semaphore_signal(
            barrier, inc=1, device_id={"space": lax.rem(s + d, space)}, device_id_type=MESH
        )

    @pl.loop(c + 1, cuts)
    def _(n):
        pl.semaphore_signal(barrier, inc=1, device_id={"cuts": n}, device_id_type=MESH)

    def remote(src, dst, send, recv, **where):
        return pltpu.make_async_remote_copy(
            src_ref=src, dst_ref=dst, send_sem=send, recv_sem=recv, device_id=where, device_id_type=MESH
        )

    def rearrange(first, stop):
        @pl.loop(first, stop)
        def _(k):
            at = pl.ds(pl.multiple_of(k * ROWS, ROWS), ROWS)
            raw_copy(k).wait()
            fields = pltpu.einshape("rqj->qrj", raw[at])
            for q in range(2):
                for t in range(space):
                    weight[t, pl.ds(q * cl, cl), at] = fields[q][:, t * cl : (t + 1) * cl].T

    for copy in inputs[:2]:
        copy.wait()
    tall = pipe_in.shape[0]
    source = lax.broadcasted_iota(jnp.int32, (LANES, fine), 0)
    target = lax.broadcasted_iota(jnp.int32, (LANES, fine), 1)
    per = LANES // REFINE
    pick = source == REFINE * (target % per) + target // LANES
    spread = jnp.dot(
        pipe_in[...].astype(jnp.float32).astype(jnp.bfloat16),
        pick.astype(jnp.float32).astype(jnp.bfloat16),
        preferred_element_type=jnp.float32,
    )
    row = lax.broadcasted_iota(jnp.int32, (tall, fine), 0)
    column = lax.broadcasted_iota(jnp.int32, (tall, fine), 1)
    spread = jnp.where(row % REFINE == (column % LANES) // per, spread, 0.0)
    gather = (
        lax.broadcasted_iota(jnp.int32, (8, tall), 0) == lax.broadcasted_iota(jnp.int32, (8, tall), 1) // REFINE
    )
    phased = jnp.dot(
        gather.astype(jnp.float32).astype(jnp.bfloat16), spread.astype(jnp.bfloat16),
        preferred_element_type=jnp.float32,
    )
    rate8 = jnp.zeros(phased.shape, jnp.float32)
    for k in range(fric_in.shape[0]):
        rate8 = jnp.where(phased == float(k), fric_in[k], rate8)

    for copy in inputs[2:]:
        copy.wait()
    for side, (v, lane0) in enumerate(((nv - 1, cl - LANES), (0, 0))):
        for f in range(2):
            edge_out[side, pl.ds(f * scen, scen)] = x_in[0, :, f, pl.ds(lane0, LANES)]
        for r in range(REFINE):
            edge_out[side, pl.ds(2 * scen + r, 1)] = rate8[v : v + 1, r * LANES : (r + 1) * LANES]

    pl.semaphore_wait(barrier, space - 1 + c)

    right, left = lax.rem(s + 1, space), lax.rem(s + space - 1, space)
    edges = [
        remote(edge_out.at[0], edge_in.at[0], edge_send.at[0], edge_recv.at[0], space=right),
        remote(edge_out.at[1], edge_in.at[1], edge_send.at[1], edge_recv.at[1], space=left),
    ]
    for copy in edges:
        copy.start()
    firsts = [
        remote(scl_in.at[0], first_scl, first_send.at[0], first_recv.at[0], cuts=0),
        remote(x_in.at[0], first_x, first_send.at[1], first_recv.at[1], cuts=0),
    ]

    @pl.when(c == 1)
    def _():
        for copy in firsts:
            copy.start()

    @pl.when(member)
    def _():
        @pl.loop(0, c)
        def _(n):
            pl.semaphore_signal(ready.at[c], inc=1, device_id={"cuts": n}, device_id_type=MESH)

    for r in range(REFINE):
        for v in range(nv):
            rates[r, :, pl.ds(v * LANES, LANES)] = jnp.broadcast_to(
                rate8[v : v + 1, r * LANES : (r + 1) * LANES], (scen, LANES)
            )

    rearrange(0, EARLY)

    for copy in edges:
        copy.wait()
    near = lax.broadcasted_iota(jnp.int32, (1, LANES), 1) < HALF
    for r in range(REFINE):
        at = pl.ds(2 * scen + r, 1)
        rates[r, :, pl.ds(cl, LANES)] = jnp.broadcast_to(
            jnp.where(near, edge_in[1, at], edge_in[0, at]), (scen, LANES)
        )
    lane = lax.broadcasted_iota(jnp.int32, (1, ext), 1)
    has_right = (s < space - 1).astype(jnp.float32)
    has_left = (s > 0).astype(jnp.float32)
    keep = jnp.where(lane < cl, 1.0, jnp.where(lane < cl + HALF, has_right, has_left))

    def extended(f):
        at = pl.ds(f * scen, scen)
        halo = jnp.where(near, edge_in[1, at], edge_in[0, at])
        return keep * jnp.concatenate([x_in[0, :, f, :], halo], axis=1)

    head, flow = extended(0), extended(1)

    def sweep(_, state):
        fwd, bwd = state
        drag = []
        for r in range(REFINE):
            q = 0.5 * (fwd[r] - bwd[r])
            drag.append(q * jnp.abs(q))
        fwd_new, bwd_new = [], []
        for r in range(REFINE):
            rate = rates[r]
            if r > 0:
                prev_f, prev_d = fwd[r - 1], drag[r - 1]
            else:
                prev_f, prev_d = pltpu.roll(fwd[-1], 1, 1), pltpu.roll(drag[-1], 1, 1)
            if r < REFINE - 1:
                next_b, next_d = bwd[r + 1], drag[r + 1]
            else:
                next_b, next_d = pltpu.roll(bwd[0], ext - 1, 1), pltpu.roll(drag[0], ext - 1, 1)
            fwd_new.append(keep * (prev_f - rate * prev_d))
            bwd_new.append(keep * (next_b + rate * next_d))
        return tuple(fwd_new), tuple(bwd_new)

    fwd, bwd = lax.fori_loop(
        0, STEPS, sweep, ((head + flow,) * REFINE, (head - flow,) * REFINE), unroll=True
    )
    fwd_sum = (fwd[0] + fwd[1] + fwd[2] + fwd[3])[:, :cl]
    bwd_sum = (bwd[0] + bwd[1] + bwd[2] + bwd[3])[:, :cl]
    mean = 0.5 / REFINE
    own[:, pl.ds(0, cl)] = mean * (fwd_sum + bwd_sum)
    own[:, pl.ds(cl, cl)] = mean * (fwd_sum - bwd_sum)

    def start_copy(p, d):
        t = lax.rem(s + d, space)
        return remote(
            start.at[p], xg.at[1, s], start_send.at[p, d], xg_recv.at[1, s], cuts=p, space=t
        )

    def dl_copy(n, p):
        return remote(pack.at[p], dl.at[n], dl_send.at[p], dl_recv.at[n], cuts=p)

    def res_copy(m, p):
        return remote(res_out.at[m], res_in.at[p], res_send.at[m], res_recv.at[p], cuts=m)

    def last_copy(d):
        at = pl.ds(c * share, share)
        return remote(
            last_out, last_in.at[s, at], last_send.at[d], last_recv.at[c, s],
            cuts=last, space=lax.rem(s + d, space),
        )

    @pl.when(c == 0)
    def _():
        for copy in firsts:
            copy.wait_recv()
        for f in range(2):
            at = pl.ds(f * cl, cl)
            u = first_scl[f, :][None] * (own[:, at] - first_x[:, f, :])
            for p in range(groups):
                start[p, :, at] = u[p * share : (p + 1) * share].astype(jnp.bfloat16)
        xg[1, s] = start[0]
        for d in range(1, space):
            start_copy(0, d).start()

        @pl.loop(1, groups)
        def _(p):
            pl.semaphore_wait(ready.at[p], 1)
            for d in range(space):
                start_copy(p, d).start()

    @pl.when(c > 0)
    def _():
        for f in range(2):
            at = pl.ds(f * cl, cl)
            for p in range(groups):
                rows = slice(p * share, (p + 1) * share)
                pack[p, pl.ds(0, share), at] = own[rows, f * cl : (f + 1) * cl]
                pack[p, pl.ds(share, share), at] = x_in[0, rows, f, :]
                pack[p, pl.ds(2 * share, 1), at] = scl_in[0, f, :][None]

        @pl.loop(0, groups)
        def _(p):
            @pl.when(p > c)
            def _():
                pl.semaphore_wait(ready.at[p], 1)

            @pl.when(p != c)
            def _():
                dl_copy(c, p).start()

            @pl.when(p == c)
            def _():
                dl[p] = pack[p]

    rearrange(EARLY, chunks)

    def apply_piece(piece, t):
        return lax.dot_general(
            piece, weight[t], (((1,), (0,)), ((), ())), preferred_element_type=jnp.float32
        )

    core = lax.rem(s, 2)

    def peer_of(j):
        return lax.bitwise_xor(s, j if j == 1 else lax.bitwise_xor(j, 1 - core))

    def group_copy(slot, j):
        return remote(
            xg.at[slot, s], xg.at[slot, s], xg_send.at[slot, j], xg_recv.at[slot, s], space=peer_of(j)
        )

    def group_wait(slot, t):
        remote(xg.at[slot, t], xg.at[slot, t], xg_send.at[slot, 0], xg_recv.at[slot, t], space=t).wait_recv()

    def dl_wait(n):
        @pl.when(n != c)
        def _():
            dl_copy(n, c).wait_recv()

    def end_of(m):
        slot = lax.rem(m, 2)
        total = apply_piece(xg[slot, s], s)
        for j in range(1, space):
            peer = peer_of(j)
            group_wait(slot, peer)
            total += apply_piece(xg[slot, peer], peer)
        return total + dl[m, pl.ds(0, share)]

    def difference(n, state):
        return dl[n, pl.ds(2 * share, 1)] * (state - dl[n, pl.ds(share, share)])

    def hand_over(m, state):
        @pl.when(m == c)
        def _():
            res_in[c] = state

        @pl.when(m != c)
        def _():
            res_out[m] = state
            res_copy(m, c).start()

    def sent(m):
        @pl.when(m > 1)
        def _():
            for j in range(1, space):
                group_copy(lax.rem(m, 2), j).wait_send()

    @pl.when(member)
    def _():
        @pl.when(c > 0)
        def _():
            group_wait(1, s)

        dl_wait(1)

        @pl.loop(1, last - 1)
        def _(m):
            dl_wait(m + 1)
            state = end_of(m)
            slot = lax.rem(m + 1, 2)
            xg[slot, s] = difference(m + 1, state).astype(jnp.bfloat16)
            for j in reversed(range(1, space)):
                group_copy(slot, j).start()
            hand_over(m, state)
            sent(m)

        dl_wait(last)
        state = end_of(last - 1)
        u = difference(last, state)
        last_out[...] = u
        for d in range(1, space):
            last_copy(d).start()

        if last < groups:
            @pl.when(c == last)
            def _():
                last_in[s, pl.ds(last * share, share)] = u

        @pl.when(c != last)
        def _():
            last_copy(0).start()

        hand_over(last - 1, state)
        sent(last - 1)

    def write(f, rows, value):
        out_ref[rows, pl.ds(f * cl, cl)] = value

    @pl.when(c == 0)
    def _():
        out_ref[...] = own[...]

    @pl.when(c == last)
    def _():
        total = own[...]
        for j in range(space):
            t = s if j == 0 else peer_of(j)
            for p in range(groups):
                @pl.when(jnp.logical_or(p != c, t != s))
                def _():
                    at = pl.ds(p * share, share)
                    remote(
                        last_out, last_in.at[t, at], last_send.at[0], last_recv.at[p, t], cuts=p, space=t
                    ).wait_recv()

            total += apply_piece(last_in[t].astype(jnp.bfloat16), t)
        out_ref[...] = total

    @pl.when(jnp.logical_and(c > 0, c < last))
    def _():
        for p in range(groups):
            @pl.when(p != c)
            def _():
                res_copy(c, p).wait_recv()

            out_ref[pl.ds(p * share, share)] = res_in[p]

    @pl.when(c == 0)
    def _():
        for d in range(1, space):
            start_copy(0, d).wait_send()

        @pl.loop(1, groups)
        def _(p):
            for d in range(space):
                start_copy(p, d).wait_send()

    @pl.when(c == 1)
    def _():
        for copy in firsts:
            copy.wait_send()

    @pl.when(c > 0)
    def _():
        @pl.loop(0, groups)
        def _(p):
            @pl.when(p != c)
            def _():
                dl_copy(c, p).wait_send()

    @pl.when(member)
    def _():
        for d in range(1, space):
            last_copy(d).wait_send()

        @pl.when(c != last)
        def _():
            last_copy(0).wait_send()

        @pl.loop(1, last)
        def _(m):
            @pl.when(m != c)
            def _():
                res_copy(m, c).wait_send()


def solution(mesh):
    cuts, space = mesh.shape["cuts"], mesh.shape["space"]

    def local(start_old, scales, propagator, pipe_of_cell, friction):
        scen, cl = start_old.shape[1], start_old.shape[3]
        cells = propagator.shape[3]
        width = 2 * cl
        groups = math.gcd(cuts, scen)
        share = scen // groups
        pipes = pipe_of_cell.reshape(-1, LANES)
        hbm = pl.BlockSpec(memory_space=pltpu.HBM)
        dma = pltpu.SemaphoreType.DMA
        edge_rows = -(-(2 * scen + REFINE) // 8) * 8
        out = pl.pallas_call(
            functools.partial(kernel, cuts, space, groups),
            out_shape=jax.ShapeDtypeStruct((scen, width), jnp.float32),
            in_specs=[hbm] * 5,
            out_specs=pl.BlockSpec(memory_space=pltpu.VMEM),
            scratch_shapes=[
                pltpu.VMEM((1, scen, 2, cl), jnp.float32),
                pltpu.VMEM((1, 2, cl), jnp.float32),
                pltpu.VMEM(pipes.shape, jnp.int32),
                pltpu.SMEM(friction.shape, jnp.float32),
                pltpu.VMEM((width, 2, cells), jnp.bfloat16),
                pltpu.VMEM((space, width, width), jnp.bfloat16),
                pltpu.VMEM((REFINE, scen, cl + LANES), jnp.float32),
                pltpu.VMEM((2, edge_rows, LANES), jnp.float32),
                pltpu.VMEM((2, edge_rows, LANES), jnp.float32),
                pltpu.VMEM((scen, 2, cl), jnp.float32),
                pltpu.VMEM((2, cl), jnp.float32),
                pltpu.VMEM((scen, width), jnp.float32),
                pltpu.VMEM((groups, 2 * share + 1, width), jnp.float32),
                pltpu.VMEM((cuts, 2 * share + 1, width), jnp.float32),
                pltpu.VMEM((groups, share, width), jnp.bfloat16),
                pltpu.VMEM((2, space, share, width), jnp.bfloat16),
                pltpu.VMEM((share, width), jnp.float32),
                pltpu.VMEM((space, scen, width), jnp.float32),
                pltpu.VMEM((cuts, share, width), jnp.float32),
                pltpu.VMEM((groups, share, width), jnp.float32),
                dma((4,)),
                dma((width // ROWS,)),
                pltpu.SemaphoreType.REGULAR((groups,)),
                dma((2,)), dma((2,)),
                dma((2,)), dma((2,)),
                dma((groups,)), dma((cuts,)),
                dma((groups, space)),
                dma((2, space)), dma((2, space)),
                dma((space,)), dma((groups, space)),
                dma((cuts,)), dma((groups,)),
            ],
            compiler_params=pltpu.CompilerParams(
                collective_id=0, has_side_effects=True, vmem_limit_bytes=48 * 2**20
            ),
        )(start_old, scales, propagator.reshape(width, 2, cells), pipes, friction)
        return out.reshape(1, scen, 2, cl)

    placed = (
        P("cuts", None, None, "space"),
        P("cuts", None, "space"),
        P(None, "space", None, None),
        P("space"),
        P(),
    )
    return jax.shard_map(
        local, mesh=mesh, in_specs=placed, out_specs=P("cuts", None, None, "space"), check_vma=False
    )
```

```python
import functools
import math

import jax
import jax.numpy as jnp
from jax import lax
from jax.experimental import pallas as pl
from jax.experimental.pallas import tpu as pltpu
from jax.sharding import PartitionSpec as P

REFINE = 4
STEPS = 16
LANES = 128
HALF = LANES // 2
ROWS = 128
GROUPS = 4
REACH = STEPS // REFINE
SIDE = LANES // 4
MESH = pl.DeviceIdType.MESH


def phases(pipes, table):
    tall = pipes.shape[0]
    per = LANES // REFINE
    lane = lax.broadcasted_iota(jnp.int32, (tall, LANES), 1)
    row = lax.broadcasted_iota(jnp.int32, (tall, LANES), 0)
    mine = row % REFINE == lane // per
    table = jnp.broadcast_to(table, (tall, LANES))
    out = []
    for r in range(REFINE):
        picked = jnp.take_along_axis(pipes, REFINE * (lane % per) + r, axis=1)
        rate = jnp.where(mine, jnp.take_along_axis(table, picked, axis=1), 0.0)
        out.append([
            jnp.sum(rate[REFINE * v : REFINE * (v + 1)], axis=0, keepdims=True) for v in range(tall // REFINE)
        ])
    return out


def advance(fwd, bwd, rates, keep=None):
    lanes = fwd[0].shape[1]
    drag = []
    for r in range(REFINE):
        q = 0.5 * (fwd[r] - bwd[r])
        drag.append(q * jnp.abs(q))
    fwd_new, bwd_new = [], []
    for r in range(REFINE):
        rate = rates[r]
        if r > 0:
            prev_f, prev_d = fwd[r - 1], drag[r - 1]
        else:
            prev_f, prev_d = pltpu.roll(fwd[-1], 1, 1), pltpu.roll(drag[-1], 1, 1)
        if r < REFINE - 1:
            next_b, next_d = bwd[r + 1], drag[r + 1]
        else:
            next_b, next_d = pltpu.roll(bwd[0], lanes - 1, 1), pltpu.roll(drag[0], lanes - 1, 1)
        f, b = prev_f - rate * prev_d, next_b + rate * next_d
        fwd_new.append(f if keep is None else keep * f)
        bwd_new.append(b if keep is None else keep * b)
    return tuple(fwd_new), tuple(bwd_new)


def coarse(fwd, bwd):
    mean = 0.5 / REFINE
    fwd_sum = fwd[0] + fwd[1] + fwd[2] + fwd[3]
    bwd_sum = bwd[0] + bwd[1] + bwd[2] + bwd[3]
    return mean * (fwd_sum + bwd_sum), mean * (fwd_sum - bwd_sum)


def kernel(
    cuts, space, groups, x_hbm, scl_hbm, prop_hbm, pipe_hbm, fric_hbm, out_ref,
    x_in, scl_in, pipe_in, fric_in, raw, weight, rates, edge_x, edge_pipe, next_x, next_scl, old_out, old_in,
    own, pack, dl, start, xg, last_out, last_in, res_out, res_in,
    in_sem, raw_sem, ready, edge_send, edge_recv, next_send, next_recv, dl_send, dl_recv,
    start_send, xg_send, xg_recv, last_send, last_recv, res_send, res_recv,
):
    c = lax.axis_index("cuts")
    s = lax.axis_index("space")
    scen, cl = x_in.shape[1], x_in.shape[3]
    width = 2 * cl
    nv = cl // LANES
    share = scen // groups
    last = cuts - 1
    chunks = raw.shape[0] // ROWS
    tall = pipe_in.shape[0]
    base = cuts - groups
    member = c >= base
    me = jnp.maximum(c - base, 0)

    barrier = pltpu.get_barrier_semaphore()
    for d in range(1, space):
        pl.semaphore_signal(
            barrier, inc=1, device_id={"space": lax.rem(s + d, space)}, device_id_type=MESH
        )

    @pl.when(c + 1 < base)
    def _():
        pl.semaphore_signal(barrier, inc=1, device_id={"cuts": c + 1}, device_id_type=MESH)

    @pl.loop(jnp.maximum(c + 1, base), cuts)
    def _(n):
        pl.semaphore_signal(barrier, inc=1, device_id={"cuts": n}, device_id_type=MESH)

    inputs = [
        pltpu.make_async_copy(pipe_hbm, pipe_in, in_sem.at[0]),
        pltpu.make_async_copy(fric_hbm, fric_in, in_sem.at[1]),
        pltpu.make_async_copy(x_hbm, x_in, in_sem.at[2]),
        pltpu.make_async_copy(scl_hbm, scl_in, in_sem.at[3]),
    ]
    for copy in inputs:
        copy.start()

    def raw_copy(k):
        at = pl.ds(pl.multiple_of(k * ROWS, ROWS), ROWS)
        return pltpu.make_async_copy(prop_hbm.at[at], raw.at[at], raw_sem.at[k])

    @pl.when(member)
    def _():
        for k in range(chunks):
            raw_copy(k).start()

    def remote(src, dst, send, recv, **where):
        return pltpu.make_async_remote_copy(
            src_ref=src, dst_ref=dst, send_sem=send, recv_sem=recv, device_id=where, device_id_type=MESH
        )

    def rearrange(first, stop):
        @pl.loop(first, stop)
        def _(k):
            at = pl.ds(pl.multiple_of(k * ROWS, ROWS), ROWS)
            raw_copy(k).wait()
            fields = pltpu.einshape("rqj->qrj", raw[at])
            for q in range(2):
                for t in range(space):
                    weight[t, pl.ds(q * cl, cl), at] = fields[q][:, t * cl : (t + 1) * cl].T

    pl.semaphore_wait(barrier, space - 1 + jnp.where(member, c, jnp.minimum(c, 1)))

    right, left = lax.rem(s + 1, space), lax.rem(s + space - 1, space)
    edges = [
        remote(pipe_hbm, edge_pipe.at[0], edge_send.at[0], edge_recv.at[0], space=right),
        remote(pipe_hbm, edge_pipe.at[1], edge_send.at[1], edge_recv.at[1], space=left),
        remote(x_hbm.at[0, :, :, pl.ds(cl - LANES, LANES)], edge_x.at[0], edge_send.at[2], edge_recv.at[2], space=right),
        remote(x_hbm.at[0, :, :, pl.ds(0, LANES)], edge_x.at[1], edge_send.at[3], edge_recv.at[3], space=left),
    ]
    for copy in edges:
        copy.start()
    before = jnp.maximum(c - 1, 0)
    nexts = [
        remote(scl_hbm.at[0], next_scl, next_send.at[0], next_recv.at[0], cuts=before),
        remote(x_hbm.at[0], next_x, next_send.at[1], next_recv.at[1], cuts=before),
    ]

    def old_copy():
        return remote(old_out, old_in, next_send.at[2], next_recv.at[2], cuts=before)

    @pl.when(c > 0)
    def _():
        nexts[0].start()

    @pl.when(c > 1)
    def _():
        nexts[1].start()

    @pl.when(member)
    def _():
        @pl.loop(0, c)
        def _(n):
            pl.semaphore_signal(ready.at[me], inc=1, device_id={"cuts": n}, device_id_type=MESH)

    for copy in inputs:
        copy.wait()

    @pl.when(c == 1)
    def _():
        for f in range(2):
            old_out[:, pl.ds(f * cl, cl)] = (scl_in[0, f, :][None] * x_in[0, :, f, :]).astype(jnp.bfloat16)
        old_copy().start()

    table = fric_in[...]
    here = phases(pipe_in[...], table)
    for r in range(REFINE):
        for v in range(nv):
            rates[r, :, pl.ds(v * LANES, LANES)] = jnp.broadcast_to(here[r][v], (scen, LANES))
    head, flow = x_in[0, :, 0, :], x_in[0, :, 1, :]
    fwd, bwd = (head + flow,) * REFINE, (head - flow,) * REFINE
    for _ in range(STEPS):
        fwd, bwd = advance(fwd, bwd, [rates[r] for r in range(REFINE)])
    for f, value in enumerate(coarse(fwd, bwd)):
        own[:, pl.ds(f * cl, cl)] = value

    @pl.when(member)
    def _():
        rearrange(0, chunks)

    for copy in edges:
        copy.wait()
    lane = lax.broadcasted_iota(jnp.int32, (1, LANES), 1)
    half = lane < HALF

    def ends(own_first, own_last, left_last, right_first):
        return jnp.where(
            half,
            pltpu.roll(jnp.where(half, right_first, own_last), SIDE, 1),
            pltpu.roll(jnp.where(half, own_first, left_last), LANES - SIDE, 1),
        )

    near = phases(
        jnp.concatenate([edge_pipe[0, pl.ds(tall - REFINE, REFINE)], edge_pipe[1, pl.ds(0, REFINE)]], axis=0), table
    )
    end_rates = [
        jnp.broadcast_to(
            ends(*(jnp.broadcast_to(v, (8, LANES)) for v in (here[r][0], here[r][-1], near[r][0], near[r][1])))[:1],
            (scen, LANES),
        )
        for r in range(REFINE)
    ]
    has_right = (s < space - 1).astype(jnp.float32)
    has_left = (s > 0).astype(jnp.float32)
    keep = jnp.where(
        lane < SIDE, 1.0, jnp.where(half, has_right, jnp.where(lane < LANES - SIDE, has_left, 1.0))
    )
    head, flow = (
        keep * ends(x_in[0, :, f, pl.ds(0, LANES)], x_in[0, :, f, pl.ds(cl - LANES, LANES)], edge_x[0, :, f, :], edge_x[1, :, f, :])
        for f in range(2)
    )
    fwd, bwd = (head + flow,) * REFINE, (head - flow,) * REFINE
    for _ in range(STEPS):
        fwd, bwd = advance(fwd, bwd, end_rates, keep)
    for f, value in enumerate(coarse(fwd, bwd)):
        first, final = pl.ds(f * cl, LANES), pl.ds((f + 1) * cl - LANES, LANES)
        own[:, first] = jnp.where(lane < REACH, pltpu.roll(value, SIDE, 1), own[:, first])
        own[:, final] = jnp.where(lane >= LANES - REACH, pltpu.roll(value, LANES - SIDE, 1), own[:, final])

    def start_copy(p, d):
        t = lax.rem(s + d, space)
        return remote(
            start.at[p], xg.at[1, s], start_send.at[p, d], xg_recv.at[1, s], cuts=base + p, space=t
        )

    def dl_copy(n, p):
        return remote(pack.at[p], dl.at[n], dl_send.at[p], dl_recv.at[n], cuts=base + p)

    def res_copy(m, p):
        return remote(res_out.at[m], res_in.at[p], res_send.at[m], res_recv.at[p], cuts=m)

    def last_copy(d):
        return remote(
            last_out, last_in.at[s, me], last_send.at[d], last_recv.at[me, s],
            cuts=last, space=lax.rem(s + d, space),
        )

    def forcing(f):
        return next_scl[f, :][None] * (own[:, pl.ds(f * cl, cl)] - next_x[:, f, :])

    @pl.when(c == 0)
    def _():
        nexts[0].wait_recv()
        old_copy().wait_recv()
        for f in range(2):
            at = pl.ds(f * cl, cl)
            u = next_scl[f, :][None] * own[:, at] - old_in[:, at].astype(jnp.float32)
            for p in range(groups):
                start[p, :, pl.ds(f * cl, cl)] = u[p * share : (p + 1) * share].astype(jnp.bfloat16)

        @pl.loop(0, groups)
        def _(p):
            pl.semaphore_wait(ready.at[p], 1)
            for d in range(space):
                start_copy(p, d).start()

    @pl.when(jnp.logical_and(c > 0, c < last))
    def _():
        for copy in nexts:
            copy.wait_recv()
        for f in range(2):
            u = forcing(f)
            for p in range(groups):
                pack[p, pl.ds(0, share), pl.ds(f * cl, cl)] = u[p * share : (p + 1) * share]
        for p in range(groups):
            pack[p, pl.ds(0, 2), pl.ds(width, cl)] = next_scl[...]

        @pl.loop(0, groups)
        def _(p):
            @pl.when(base + p > c)
            def _():
                pl.semaphore_wait(ready.at[p], 1)

            @pl.when(base + p != c)
            def _():
                dl_copy(c, p).start()

            @pl.when(base + p == c)
            def _():
                dl[base + p] = pack[p]

    def apply_piece(piece, t):
        return lax.dot_general(
            piece, weight[t], (((1,), (0,)), ((), ())), preferred_element_type=jnp.float32
        )

    core = lax.rem(s, 2)

    def peer_of(j):
        return lax.bitwise_xor(s, j if j == 1 else lax.bitwise_xor(j, 1 - core))

    def group_copy(slot, j):
        return remote(
            xg.at[slot, s], xg.at[slot, s], xg_send.at[slot, j], xg_recv.at[slot, s], space=peer_of(j)
        )

    def group_wait(slot, t):
        remote(xg.at[slot, t], xg.at[slot, t], xg_send.at[slot, 0], xg_recv.at[slot, t], space=t).wait_recv()

    def image_of(m):
        slot = lax.rem(m, 2)
        total = apply_piece(xg[slot, s], s)
        for j in range(1, space):
            peer = peer_of(j)
            group_wait(slot, peer)
            total += apply_piece(xg[slot, peer], peer)

        @pl.when(m != c)
        def _():
            dl_copy(m, me).wait_recv()

        return total

    def difference(m, image, f):
        return dl[m, pl.ds(f, 1), pl.ds(width, cl)] * image[:, f * cl : (f + 1) * cl] + dl[
            m, pl.ds(0, share), pl.ds(f * cl, cl)
        ]

    def hand_over(m, image):
        @pl.when(m == c)
        def _():
            res_in[me] = image

        @pl.when(m != c)
        def _():
            res_out[m] = image
            res_copy(m, me).start()

    def sent(m):
        @pl.when(m > 1)
        def _():
            for j in range(1, space):
                group_copy(lax.rem(m, 2), j).wait_send()

    @pl.when(member)
    def _():
        group_wait(1, s)

        @pl.loop(1, last - 1)
        def _(m):
            image = image_of(m)
            slot = lax.rem(m + 1, 2)
            for f in range(2):
                xg[slot, s, :, pl.ds(f * cl, cl)] = difference(m, image, f).astype(jnp.bfloat16)
            for j in reversed(range(1, space)):
                group_copy(slot, j).start()
            hand_over(m, image)
            sent(m)

        image = image_of(last - 1)
        for f in range(2):
            last_out[:, pl.ds(f * cl, cl)] = difference(last - 1, image, f).astype(jnp.bfloat16)
        for d in range(1, space):
            last_copy(d).start()

        @pl.when(c == last)
        def _():
            last_in[s, groups - 1] = last_out[...]

        @pl.when(c != last)
        def _():
            last_copy(0).start()

        hand_over(last - 1, image)
        sent(last - 1)

    @pl.when(c == 0)
    def _():
        out_ref[...] = own[...]

    @pl.when(c == last)
    def _():
        total = own[...]
        for t in [*range(1, space, 2), *range(0, space, 2)]:
            for p in range(groups):
                @pl.when(jnp.logical_or(base + p != c, t != s))
                def _():
                    remote(
                        last_out, last_in.at[t, p], last_send.at[0], last_recv.at[p, t], cuts=base + p, space=t
                    ).wait_recv()

            piece = jnp.concatenate([last_in[t, p].astype(jnp.float32) for p in range(groups)], axis=0)
            total += apply_piece(piece.astype(jnp.bfloat16), t)
        out_ref[...] = total

    @pl.when(jnp.logical_and(c > 0, c < last))
    def _():
        for p in range(groups):
            @pl.when(base + p != c)
            def _():
                res_copy(c, p).wait_recv()

            at = pl.ds(p * share, share)
            out_ref[at] = res_in[p] + own[at]

    @pl.when(c == 0)
    def _():
        @pl.loop(0, groups)
        def _(p):
            for d in range(space):
                start_copy(p, d).wait_send()

    @pl.when(c > 0)
    def _():
        nexts[0].wait_send()

    @pl.when(c == 1)
    def _():
        old_copy().wait_send()

    @pl.when(c > 1)
    def _():
        nexts[1].wait_send()

    @pl.when(jnp.logical_and(c > 0, c < last))
    def _():
        @pl.loop(0, groups)
        def _(p):
            @pl.when(base + p != c)
            def _():
                dl_copy(c, p).wait_send()

    @pl.when(member)
    def _():
        for d in range(1, space):
            last_copy(d).wait_send()

        @pl.when(c != last)
        def _():
            last_copy(0).wait_send()

        @pl.loop(1, last)
        def _(m):
            @pl.when(m != c)
            def _():
                res_copy(m, me).wait_send()


def solution(mesh):
    cuts, space = mesh.shape["cuts"], mesh.shape["space"]

    def local(start_old, scales, propagator, pipe_of_cell, friction):
        scen, cl = start_old.shape[1], start_old.shape[3]
        cells = propagator.shape[3]
        width = 2 * cl
        groups = math.gcd(GROUPS, math.gcd(cuts, scen))
        share = scen // groups
        pipes = pipe_of_cell.reshape(-1, LANES)
        hbm = pl.BlockSpec(memory_space=pltpu.HBM)
        dma = pltpu.SemaphoreType.DMA
        out = pl.pallas_call(
            functools.partial(kernel, cuts, space, groups),
            out_shape=jax.ShapeDtypeStruct((scen, width), jnp.float32),
            in_specs=[hbm] * 5,
            out_specs=pl.BlockSpec(memory_space=pltpu.VMEM),
            scratch_shapes=[
                pltpu.VMEM((1, scen, 2, cl), jnp.float32),
                pltpu.VMEM((1, 2, cl), jnp.float32),
                pltpu.VMEM(pipes.shape, jnp.int32),
                pltpu.VMEM((1, LANES), jnp.float32),
                pltpu.VMEM((width, 2, cells), jnp.bfloat16),
                pltpu.VMEM((space, width, width), jnp.bfloat16),
                pltpu.VMEM((REFINE, scen, cl), jnp.float32),
                pltpu.VMEM((2, scen, 2, LANES), jnp.float32),
                pltpu.VMEM((2,) + pipes.shape, jnp.int32),
                pltpu.VMEM((scen, 2, cl), jnp.float32),
                pltpu.VMEM((2, cl), jnp.float32),
                pltpu.VMEM((scen, width), jnp.bfloat16),
                pltpu.VMEM((scen, width), jnp.bfloat16),
                pltpu.VMEM((scen, width), jnp.float32),
                pltpu.VMEM((groups, max(share, 2), width + cl), jnp.float32),
                pltpu.VMEM((cuts, max(share, 2), width + cl), jnp.float32),
                pltpu.VMEM((groups, share, width), jnp.bfloat16),
                pltpu.VMEM((2, space, share, width), jnp.bfloat16),
                pltpu.VMEM((share, width), jnp.bfloat16),
                pltpu.VMEM((space, groups, share, width), jnp.bfloat16),
                pltpu.VMEM((cuts, share, width), jnp.float32),
                pltpu.VMEM((groups, share, width), jnp.float32),
                dma((4,)),
                dma((width // ROWS,)),
                pltpu.SemaphoreType.REGULAR((groups,)),
                dma((4,)), dma((4,)),
                dma((3,)), dma((3,)),
                dma((groups,)), dma((cuts,)),
                dma((groups, space)),
                dma((2, space)), dma((2, space)),
                dma((space,)), dma((groups, space)),
                dma((cuts,)), dma((groups,)),
            ],
            compiler_params=pltpu.CompilerParams(
                collective_id=0, has_side_effects=True, vmem_limit_bytes=60 * 2**20
            ),
        )(start_old, scales, propagator.reshape(width, 2, cells), pipes, friction.reshape(1, -1))
        return out.reshape(1, scen, 2, cl)

    placed = (
        P("cuts", None, None, "space"),
        P("cuts", None, "space"),
        P(None, "space", None, None),
        P("space"),
        P(),
    )
    return jax.shard_map(
        local, mesh=mesh, in_specs=placed, out_specs=P("cuts", None, None, "space"), check_vma=False
    )
```

```python
import functools
import math

import jax
import jax.numpy as jnp
from jax import lax
from jax.experimental import pallas as pl
from jax.experimental.pallas import tpu as pltpu
from jax.sharding import PartitionSpec as P

REFINE = 4
STEPS = 16
LANES = 128
HALF = LANES // 2
ROWS = 128
GROUPS = 4
REACH = STEPS // REFINE
SIDE = LANES // 4
MESH = pl.DeviceIdType.MESH


def phases(pipes, table):
    tall = pipes.shape[0]
    per = LANES // REFINE
    lane = lax.broadcasted_iota(jnp.int32, (tall, LANES), 1)
    row = lax.broadcasted_iota(jnp.int32, (tall, LANES), 0)
    mine = row % REFINE == lane // per
    table = jnp.broadcast_to(table, (tall, LANES))
    out = []
    for r in range(REFINE):
        picked = jnp.take_along_axis(pipes, REFINE * (lane % per) + r, axis=1)
        rate = jnp.where(mine, jnp.take_along_axis(table, picked, axis=1), 0.0)
        out.append([
            jnp.sum(rate[REFINE * v : REFINE * (v + 1)], axis=0, keepdims=True) for v in range(tall // REFINE)
        ])
    return out


def neighbours(values):
    lanes = values[0].shape[-1]

    def rolled(v, by):
        return pltpu.roll(v.reshape(-1, lanes), by, 1).reshape(v.shape)

    return [rolled(v, 1) for v in values] + list(values) + [rolled(v, lanes - 1) for v in values]


def advance_phases(fwd, bwd, rates, keeps):
    fwd, bwd = neighbours(fwd), neighbours(bwd)
    for step in range(REFINE):
        drag = {}
        for i in range(step, 3 * REFINE - step):
            q = 0.5 * (fwd[i] - bwd[i])
            drag[i] = q * jnp.abs(q)
        fwd_new, bwd_new = list(fwd), list(bwd)
        for i in range(step + 1, 3 * REFINE - step - 1):
            fwd_new[i] = keeps[i] * (fwd[i - 1] - rates[i] * drag[i - 1])
            bwd_new[i] = keeps[i] * (bwd[i + 1] + rates[i] * drag[i + 1])
        fwd, bwd = fwd_new, bwd_new
    return tuple(fwd[REFINE : 2 * REFINE]), tuple(bwd[REFINE : 2 * REFINE])


def advance(fwd, bwd, rates):
    lanes = fwd[0].shape[1]
    drag = []
    for r in range(REFINE):
        q = 0.5 * (fwd[r] - bwd[r])
        drag.append(q * jnp.abs(q))
    fwd_new, bwd_new = [], []
    for r in range(REFINE):
        rate = rates[r]
        if r > 0:
            prev_f, prev_d = fwd[r - 1], drag[r - 1]
        else:
            prev_f, prev_d = pltpu.roll(fwd[-1], 1, 1), pltpu.roll(drag[-1], 1, 1)
        if r < REFINE - 1:
            next_b, next_d = bwd[r + 1], drag[r + 1]
        else:
            next_b, next_d = pltpu.roll(bwd[0], lanes - 1, 1), pltpu.roll(drag[0], lanes - 1, 1)
        fwd_new.append(prev_f - rate * prev_d)
        bwd_new.append(next_b + rate * next_d)
    return tuple(fwd_new), tuple(bwd_new)


def coarse(fwd, bwd):
    mean = 0.5 / REFINE
    fwd_sum = fwd[0] + fwd[1] + fwd[2] + fwd[3]
    bwd_sum = bwd[0] + bwd[1] + bwd[2] + bwd[3]
    return mean * (fwd_sum + bwd_sum), mean * (fwd_sum - bwd_sum)


def kernel(
    cuts, space, groups, x_hbm, scl_hbm, prop_hbm, pipe_hbm, fric_hbm, out_ref,
    x_in, scl_in, pipe_in, fric_in, raw, weight, rates, edge_x, edge_pipe, next_x, next_scl, old_out, old_in,
    own, pack, dl, start, xg, last_out, last_in, res_out, res_in,
    in_sem, raw_sem, ready, edge_send, edge_recv, next_send, next_recv, dl_send, dl_recv,
    start_send, xg_send, xg_recv, last_send, last_recv, res_send, res_recv,
):
    c = lax.axis_index("cuts")
    s = lax.axis_index("space")
    scen, cl = x_in.shape[1], x_in.shape[3]
    width = 2 * cl
    nv = cl // LANES
    share = scen // groups
    last = cuts - 1
    chunks = raw.shape[0] // ROWS
    tall = pipe_in.shape[0]
    base = cuts - groups
    member = c >= base
    me = jnp.maximum(c - base, 0)

    barrier = pltpu.get_barrier_semaphore()
    for d in range(1, space):
        pl.semaphore_signal(
            barrier, inc=1, device_id={"space": lax.rem(s + d, space)}, device_id_type=MESH
        )

    @pl.when(c + 1 < base)
    def _():
        pl.semaphore_signal(barrier, inc=1, device_id={"cuts": c + 1}, device_id_type=MESH)

    @pl.loop(jnp.maximum(c + 1, base), cuts)
    def _(n):
        pl.semaphore_signal(barrier, inc=1, device_id={"cuts": n}, device_id_type=MESH)

    inputs = [
        pltpu.make_async_copy(pipe_hbm, pipe_in, in_sem.at[0]),
        pltpu.make_async_copy(fric_hbm, fric_in, in_sem.at[1]),
        pltpu.make_async_copy(x_hbm, x_in, in_sem.at[2]),
        pltpu.make_async_copy(scl_hbm, scl_in, in_sem.at[3]),
    ]
    for copy in inputs:
        copy.start()

    def raw_copy(k):
        at = pl.ds(pl.multiple_of(k * ROWS, ROWS), ROWS)
        return pltpu.make_async_copy(prop_hbm.at[at], raw.at[at], raw_sem.at[k])

    @pl.when(member)
    def _():
        for k in range(chunks):
            raw_copy(k).start()

    def remote(src, dst, send, recv, **where):
        return pltpu.make_async_remote_copy(
            src_ref=src, dst_ref=dst, send_sem=send, recv_sem=recv, device_id=where, device_id_type=MESH
        )

    def rearrange(first, stop):
        @pl.loop(first, stop)
        def _(k):
            at = pl.ds(pl.multiple_of(k * ROWS, ROWS), ROWS)
            raw_copy(k).wait()
            fields = pltpu.einshape("rqj->qrj", raw[at])
            for q in range(2):
                for t in range(space):
                    weight[t, pl.ds(q * cl, cl), at] = fields[q][:, t * cl : (t + 1) * cl].T

    pl.semaphore_wait(barrier, space - 1 + jnp.where(member, c, jnp.minimum(c, 1)))

    right, left = lax.rem(s + 1, space), lax.rem(s + space - 1, space)
    edges = [
        remote(pipe_hbm, edge_pipe.at[0], edge_send.at[0], edge_recv.at[0], space=right),
        remote(pipe_hbm, edge_pipe.at[1], edge_send.at[1], edge_recv.at[1], space=left),
        remote(x_hbm.at[0, :, :, pl.ds(cl - LANES, LANES)], edge_x.at[0], edge_send.at[2], edge_recv.at[2], space=right),
        remote(x_hbm.at[0, :, :, pl.ds(0, LANES)], edge_x.at[1], edge_send.at[3], edge_recv.at[3], space=left),
    ]
    for copy in edges:
        copy.start()
    before = jnp.maximum(c - 1, 0)
    nexts = [
        remote(scl_hbm.at[0], next_scl, next_send.at[0], next_recv.at[0], cuts=before),
        remote(x_hbm.at[0], next_x, next_send.at[1], next_recv.at[1], cuts=before),
    ]

    def old_copy():
        return remote(old_out, old_in, next_send.at[2], next_recv.at[2], cuts=before)

    @pl.when(c > 0)
    def _():
        nexts[0].start()

    @pl.when(c > 1)
    def _():
        nexts[1].start()

    @pl.when(member)
    def _():
        @pl.loop(0, c)
        def _(n):
            pl.semaphore_signal(ready.at[me], inc=1, device_id={"cuts": n}, device_id_type=MESH)

    for copy in inputs:
        copy.wait()

    @pl.when(c == 1)
    def _():
        for f in range(2):
            old_out[:, pl.ds(f * cl, cl)] = (scl_in[0, f, :][None] * x_in[0, :, f, :]).astype(jnp.bfloat16)
        old_copy().start()

    table = fric_in[...]
    here = phases(pipe_in[...], table)
    for r in range(REFINE):
        for v in range(nv):
            rates[r, :, pl.ds(v * LANES, LANES)] = jnp.broadcast_to(here[r][v], (scen, LANES))
    head, flow = x_in[0, :, 0, :], x_in[0, :, 1, :]
    fwd, bwd = (head + flow,) * REFINE, (head - flow,) * REFINE
    for _ in range(STEPS):
        fwd, bwd = advance(fwd, bwd, [rates[r] for r in range(REFINE)])
    for f, value in enumerate(coarse(fwd, bwd)):
        own[:, pl.ds(f * cl, cl)] = value

    @pl.when(member)
    def _():
        rearrange(0, chunks)

    for copy in edges:
        copy.wait()
    lane = lax.broadcasted_iota(jnp.int32, (1, LANES), 1)
    half = lane < HALF

    def ends(own_first, own_last, left_last, right_first):
        return jnp.where(
            half,
            pltpu.roll(jnp.where(half, right_first, own_last), SIDE, 1),
            pltpu.roll(jnp.where(half, own_first, left_last), LANES - SIDE, 1),
        )

    near = phases(
        jnp.concatenate([edge_pipe[0, pl.ds(tall - REFINE, REFINE)], edge_pipe[1, pl.ds(0, REFINE)]], axis=0), table
    )
    end_rates = [
        ends(*(jnp.broadcast_to(v, (8, LANES)) for v in (here[r][0], here[r][-1], near[r][0], near[r][1])))
        for r in range(REFINE)
    ]
    has_right = (s < space - 1).astype(jnp.float32)
    has_left = (s > 0).astype(jnp.float32)
    keep = jnp.where(
        lane < SIDE, 1.0, jnp.where(half, has_right, jnp.where(lane < LANES - SIDE, has_left, 1.0))
    )
    head, flow = (
        keep * ends(x_in[0, :, f, pl.ds(0, LANES)], x_in[0, :, f, pl.ds(cl - LANES, LANES)], edge_x[0, :, f, :], edge_x[1, :, f, :])
        for f in range(2)
    )
    head, flow = head.reshape(-1, 8, LANES), flow.reshape(-1, 8, LANES)
    fwd, bwd = (head + flow,) * REFINE, (head - flow,) * REFINE
    end_rates, keeps = neighbours(end_rates), neighbours([jnp.broadcast_to(keep, (8, LANES))] * REFINE)
    for _ in range(STEPS // REFINE):
        fwd, bwd = advance_phases(fwd, bwd, end_rates, keeps)
    for f, value in enumerate(coarse(fwd, bwd)):
        value = value.reshape(scen, LANES)
        first, final = pl.ds(f * cl, LANES), pl.ds((f + 1) * cl - LANES, LANES)
        own[:, first] = jnp.where(lane < REACH, pltpu.roll(value, SIDE, 1), own[:, first])
        own[:, final] = jnp.where(lane >= LANES - REACH, pltpu.roll(value, LANES - SIDE, 1), own[:, final])

    def start_copy(p, d):
        t = lax.rem(s + d, space)
        return remote(
            start.at[p], xg.at[1, s], start_send.at[p, d], xg_recv.at[1, s], cuts=base + p, space=t
        )

    def dl_copy(n, p):
        return remote(pack.at[p], dl.at[n], dl_send.at[p], dl_recv.at[n], cuts=base + p)

    def res_copy(m, p):
        return remote(res_out.at[m], res_in.at[p], res_send.at[m], res_recv.at[p], cuts=m)

    def last_copy(d):
        return remote(
            last_out, last_in.at[s, me], last_send.at[d], last_recv.at[me, s],
            cuts=last, space=lax.rem(s + d, space),
        )

    def forcing(f):
        return next_scl[f, :][None] * (own[:, pl.ds(f * cl, cl)] - next_x[:, f, :])

    @pl.when(c == 0)
    def _():
        nexts[0].wait_recv()
        old_copy().wait_recv()
        for f in range(2):
            at = pl.ds(f * cl, cl)
            u = next_scl[f, :][None] * own[:, at] - old_in[:, at].astype(jnp.float32)
            for p in range(groups):
                start[p, :, pl.ds(f * cl, cl)] = u[p * share : (p + 1) * share].astype(jnp.bfloat16)

        @pl.loop(0, groups)
        def _(p):
            pl.semaphore_wait(ready.at[p], 1)
            for d in range(space):
                start_copy(p, d).start()

    @pl.when(jnp.logical_and(c > 0, c < last))
    def _():
        for copy in nexts:
            copy.wait_recv()
        for f in range(2):
            u = forcing(f)
            for p in range(groups):
                pack[p, pl.ds(0, share), pl.ds(f * cl, cl)] = u[p * share : (p + 1) * share]
        for p in range(groups):
            pack[p, pl.ds(0, 2), pl.ds(width, cl)] = next_scl[...]

        @pl.loop(0, groups)
        def _(p):
            @pl.when(base + p > c)
            def _():
                pl.semaphore_wait(ready.at[p], 1)

            @pl.when(base + p != c)
            def _():
                dl_copy(c, p).start()

            @pl.when(base + p == c)
            def _():
                dl[base + p] = pack[p]

    def apply_piece(piece, t):
        return lax.dot_general(
            piece, weight[t], (((1,), (0,)), ((), ())), preferred_element_type=jnp.float32
        )

    core = lax.rem(s, 2)

    def peer_of(j):
        return lax.bitwise_xor(s, j if j == 1 else lax.bitwise_xor(j, 1 - core))

    def group_copy(slot, j):
        return remote(
            xg.at[slot, s], xg.at[slot, s], xg_send.at[slot, j], xg_recv.at[slot, s], space=peer_of(j)
        )

    def group_wait(slot, t):
        remote(xg.at[slot, t], xg.at[slot, t], xg_send.at[slot, 0], xg_recv.at[slot, t], space=t).wait_recv()

    def image_of(m):
        slot = lax.rem(m, 2)
        total = apply_piece(xg[slot, s], s)
        for j in range(1, space):
            peer = peer_of(j)
            group_wait(slot, peer)
            total += apply_piece(xg[slot, peer], peer)

        @pl.when(m != c)
        def _():
            dl_copy(m, me).wait_recv()

        return total

    def difference(m, image, f):
        return dl[m, pl.ds(f, 1), pl.ds(width, cl)] * image[:, f * cl : (f + 1) * cl] + dl[
            m, pl.ds(0, share), pl.ds(f * cl, cl)
        ]

    def hand_over(m, image):
        @pl.when(m == c)
        def _():
            res_in[me] = image

        @pl.when(m != c)
        def _():
            res_out[m] = image
            res_copy(m, me).start()

    def sent(m):
        @pl.when(m > 1)
        def _():
            for j in range(1, space):
                group_copy(lax.rem(m, 2), j).wait_send()

    @pl.when(member)
    def _():
        group_wait(1, s)

        @pl.loop(1, last - 1)
        def _(m):
            image = image_of(m)
            slot = lax.rem(m + 1, 2)
            for f in range(2):
                xg[slot, s, :, pl.ds(f * cl, cl)] = difference(m, image, f).astype(jnp.bfloat16)
            for j in reversed(range(1, space)):
                group_copy(slot, j).start()
            hand_over(m, image)
            sent(m)

        image = image_of(last - 1)
        for f in range(2):
            last_out[:, pl.ds(f * cl, cl)] = difference(last - 1, image, f).astype(jnp.bfloat16)
        for d in range(1, space):
            last_copy(d).start()

        @pl.when(c == last)
        def _():
            last_in[s, groups - 1] = last_out[...]

        @pl.when(c != last)
        def _():
            last_copy(0).start()

        hand_over(last - 1, image)
        sent(last - 1)

    @pl.when(c == 0)
    def _():
        out_ref[...] = own[...]

    @pl.when(c == last)
    def _():
        total = own[...]
        for t in [*range(1, space, 2), *range(0, space, 2)]:
            for p in range(groups):
                @pl.when(jnp.logical_or(base + p != c, t != s))
                def _():
                    remote(
                        last_out, last_in.at[t, p], last_send.at[0], last_recv.at[p, t], cuts=base + p, space=t
                    ).wait_recv()

            piece = jnp.concatenate([last_in[t, p].astype(jnp.float32) for p in range(groups)], axis=0)
            total += apply_piece(piece.astype(jnp.bfloat16), t)
        out_ref[...] = total

    @pl.when(jnp.logical_and(c > 0, c < last))
    def _():
        for p in range(groups):
            @pl.when(base + p != c)
            def _():
                res_copy(c, p).wait_recv()

            at = pl.ds(p * share, share)
            out_ref[at] = res_in[p] + own[at]

    @pl.when(c == 0)
    def _():
        @pl.loop(0, groups)
        def _(p):
            for d in range(space):
                start_copy(p, d).wait_send()

    @pl.when(c > 0)
    def _():
        nexts[0].wait_send()

    @pl.when(c == 1)
    def _():
        old_copy().wait_send()

    @pl.when(c > 1)
    def _():
        nexts[1].wait_send()

    @pl.when(jnp.logical_and(c > 0, c < last))
    def _():
        @pl.loop(0, groups)
        def _(p):
            @pl.when(base + p != c)
            def _():
                dl_copy(c, p).wait_send()

    @pl.when(member)
    def _():
        for d in range(1, space):
            last_copy(d).wait_send()

        @pl.when(c != last)
        def _():
            last_copy(0).wait_send()

        @pl.loop(1, last)
        def _(m):
            @pl.when(m != c)
            def _():
                res_copy(m, me).wait_send()


def solution(mesh):
    cuts, space = mesh.shape["cuts"], mesh.shape["space"]

    def local(start_old, scales, propagator, pipe_of_cell, friction):
        scen, cl = start_old.shape[1], start_old.shape[3]
        cells = propagator.shape[3]
        width = 2 * cl
        groups = math.gcd(GROUPS, math.gcd(cuts, scen))
        share = scen // groups
        pipes = pipe_of_cell.reshape(-1, LANES)
        hbm = pl.BlockSpec(memory_space=pltpu.HBM)
        dma = pltpu.SemaphoreType.DMA
        out = pl.pallas_call(
            functools.partial(kernel, cuts, space, groups),
            out_shape=pltpu.VMEM((scen, width), jnp.float32),
            in_specs=[hbm] * 5,
            out_specs=pl.BlockSpec(memory_space=pltpu.VMEM),
            scratch_shapes=[
                pltpu.VMEM((1, scen, 2, cl), jnp.float32),
                pltpu.VMEM((1, 2, cl), jnp.float32),
                pltpu.VMEM(pipes.shape, jnp.int32),
                pltpu.VMEM((1, LANES), jnp.float32),
                pltpu.VMEM((width, 2, cells), jnp.bfloat16),
                pltpu.VMEM((space, width, width), jnp.bfloat16),
                pltpu.VMEM((REFINE, scen, cl), jnp.float32),
                pltpu.VMEM((2, scen, 2, LANES), jnp.float32),
                pltpu.VMEM((2,) + pipes.shape, jnp.int32),
                pltpu.VMEM((scen, 2, cl), jnp.float32),
                pltpu.VMEM((2, cl), jnp.float32),
                pltpu.VMEM((scen, width), jnp.bfloat16),
                pltpu.VMEM((scen, width), jnp.bfloat16),
                pltpu.VMEM((scen, width), jnp.float32),
                pltpu.VMEM((groups, max(share, 2), width + cl), jnp.float32),
                pltpu.VMEM((cuts, max(share, 2), width + cl), jnp.float32),
                pltpu.VMEM((groups, share, width), jnp.bfloat16),
                pltpu.VMEM((2, space, share, width), jnp.bfloat16),
                pltpu.VMEM((share, width), jnp.bfloat16),
                pltpu.VMEM((space, groups, share, width), jnp.bfloat16),
                pltpu.VMEM((cuts, share, width), jnp.float32),
                pltpu.VMEM((groups, share, width), jnp.float32),
                dma((4,)),
                dma((width // ROWS,)),
                pltpu.SemaphoreType.REGULAR((groups,)),
                dma((4,)), dma((4,)),
                dma((3,)), dma((3,)),
                dma((groups,)), dma((cuts,)),
                dma((groups, space)),
                dma((2, space)), dma((2, space)),
                dma((space,)), dma((groups, space)),
                dma((cuts,)), dma((groups,)),
            ],
            compiler_params=pltpu.CompilerParams(
                collective_id=0, has_side_effects=True, vmem_limit_bytes=60 * 2**20
            ),
        )(start_old, scales, propagator.reshape(width, 2, cells), pipes, friction.reshape(1, -1))
        return out.reshape(1, scen, 2, cl)

    placed = (
        P("cuts", None, None, "space"),
        P("cuts", None, "space"),
        P(None, "space", None, None),
        P("space"),
        P(),
    )
    return jax.shard_map(
        local, mesh=mesh, in_specs=placed, out_specs=P("cuts", None, None, "space"), check_vma=False
    )
```

```python
import functools
import math

import jax
import jax.numpy as jnp
from jax import lax
from jax.experimental import pallas as pl
from jax.experimental.pallas import tpu as pltpu
from jax.sharding import PartitionSpec as P

REFINE = 4
STEPS = 16
LANES = 128
HALF = LANES // 2
ROWS = 128
GROUPS = 4
REACH = STEPS // REFINE
SIDE = LANES // 4
MESH = pl.DeviceIdType.MESH


def phases(pipes, table):
    tall = pipes.shape[0]
    per = LANES // REFINE
    lane = lax.broadcasted_iota(jnp.int32, (tall, LANES), 1)
    row = lax.broadcasted_iota(jnp.int32, (tall, LANES), 0)
    mine = row % REFINE == lane // per
    table = jnp.broadcast_to(table, (tall, LANES))
    out = []
    for r in range(REFINE):
        picked = jnp.take_along_axis(pipes, REFINE * (lane % per) + r, axis=1)
        rate = jnp.where(mine, jnp.take_along_axis(table, picked, axis=1), 0.0)
        out.append([
            jnp.sum(rate[REFINE * v : REFINE * (v + 1)], axis=0, keepdims=True) for v in range(tall // REFINE)
        ])
    return out


def neighbours(values):
    lanes = values[0].shape[-1]

    def rolled(v, by):
        return pltpu.roll(v.reshape(-1, lanes), by, 1).reshape(v.shape)

    return [rolled(v, 1) for v in values] + list(values) + [rolled(v, lanes - 1) for v in values]


def advance_phases(fwd, bwd, rates, keeps):
    fwd, bwd = neighbours(fwd), neighbours(bwd)
    for step in range(REFINE):
        drag = {}
        for i in range(step, 3 * REFINE - step):
            q = 0.5 * (fwd[i] - bwd[i])
            drag[i] = q * jnp.abs(q)
        fwd_new, bwd_new = list(fwd), list(bwd)
        for i in range(step + 1, 3 * REFINE - step - 1):
            fwd_new[i] = keeps[i] * (fwd[i - 1] - rates[i] * drag[i - 1])
            bwd_new[i] = keeps[i] * (bwd[i + 1] + rates[i] * drag[i + 1])
        fwd, bwd = fwd_new, bwd_new
    return tuple(fwd[REFINE : 2 * REFINE]), tuple(bwd[REFINE : 2 * REFINE])


def advance(fwd, bwd, rates):
    lanes = fwd[0].shape[1]
    drag = []
    for r in range(REFINE):
        q = 0.5 * (fwd[r] - bwd[r])
        drag.append(q * jnp.abs(q))
    fwd_new, bwd_new = [], []
    for r in range(REFINE):
        rate = rates[r]
        if r > 0:
            prev_f, prev_d = fwd[r - 1], drag[r - 1]
        else:
            prev_f, prev_d = pltpu.roll(fwd[-1], 1, 1), pltpu.roll(drag[-1], 1, 1)
        if r < REFINE - 1:
            next_b, next_d = bwd[r + 1], drag[r + 1]
        else:
            next_b, next_d = pltpu.roll(bwd[0], lanes - 1, 1), pltpu.roll(drag[0], lanes - 1, 1)
        fwd_new.append(prev_f - rate * prev_d)
        bwd_new.append(next_b + rate * next_d)
    return tuple(fwd_new), tuple(bwd_new)


def coarse(fwd, bwd):
    mean = 0.5 / REFINE
    fwd_sum = fwd[0] + fwd[1] + fwd[2] + fwd[3]
    bwd_sum = bwd[0] + bwd[1] + bwd[2] + bwd[3]
    return mean * (fwd_sum + bwd_sum), mean * (fwd_sum - bwd_sum)


def kernel(
    cuts, space, groups, x_hbm, scl_hbm, prop_hbm, pipe_hbm, fric_hbm, out_ref,
    x_in, scl_in, pipe_in, fric_in, raw, weight, rates, edge_x, edge_pipe, next_x, next_scl, old_out, old_in,
    own, pack, dl, start, xg, last_out, last_in, res_out, res_in,
    in_sem, raw_sem, ready, edge_send, edge_recv, next_send, next_recv, dl_send, dl_recv,
    start_send, start_recv, xg_send, xg_recv, last_send, last_recv, res_send, res_recv,
):
    c = lax.axis_index("cuts")
    s = lax.axis_index("space")
    scen, cl = x_in.shape[1], x_in.shape[3]
    width = 2 * cl
    nv = cl // LANES
    share = scen // groups
    last = cuts - 1
    chunks = raw.shape[0] // ROWS
    tall = pipe_in.shape[0]
    base = cuts - groups
    member = c >= base
    me = jnp.maximum(c - base, 0)

    barrier = pltpu.get_barrier_semaphore()
    for d in range(1, space):
        pl.semaphore_signal(
            barrier, inc=1, device_id={"space": lax.rem(s + d, space)}, device_id_type=MESH
        )

    @pl.when(c + 1 < base)
    def _():
        pl.semaphore_signal(barrier, inc=1, device_id={"cuts": c + 1}, device_id_type=MESH)

    @pl.loop(jnp.maximum(c + 1, base), cuts)
    def _(n):
        pl.semaphore_signal(barrier, inc=1, device_id={"cuts": n}, device_id_type=MESH)

    inputs = [
        pltpu.make_async_copy(pipe_hbm, pipe_in, in_sem.at[0]),
        pltpu.make_async_copy(fric_hbm, fric_in, in_sem.at[1]),
        pltpu.make_async_copy(x_hbm, x_in, in_sem.at[2]),
        pltpu.make_async_copy(scl_hbm, scl_in, in_sem.at[3]),
    ]
    for copy in inputs:
        copy.start()

    def raw_copy(k):
        at = pl.ds(pl.multiple_of(k * ROWS, ROWS), ROWS)
        return pltpu.make_async_copy(prop_hbm.at[at], raw.at[at], raw_sem.at[k])

    @pl.when(member)
    def _():
        for k in range(chunks):
            raw_copy(k).start()

    def remote(src, dst, send, recv, **where):
        return pltpu.make_async_remote_copy(
            src_ref=src, dst_ref=dst, send_sem=send, recv_sem=recv, device_id=where, device_id_type=MESH
        )

    def rearrange(first, stop):
        @pl.loop(first, stop)
        def _(k):
            at = pl.ds(pl.multiple_of(k * ROWS, ROWS), ROWS)
            raw_copy(k).wait()
            fields = pltpu.einshape("rqj->qrj", raw[at])
            for q in range(2):
                for t in range(space):
                    weight[t, pl.ds(q * cl, cl), at] = fields[q][:, t * cl : (t + 1) * cl].T

    pl.semaphore_wait(barrier, space - 1 + jnp.where(member, c, jnp.minimum(c, 1)))

    right, left = lax.rem(s + 1, space), lax.rem(s + space - 1, space)
    edges = [
        remote(pipe_hbm, edge_pipe.at[0], edge_send.at[0], edge_recv.at[0], space=right),
        remote(pipe_hbm, edge_pipe.at[1], edge_send.at[1], edge_recv.at[1], space=left),
        remote(x_hbm.at[0, :, :, pl.ds(cl - LANES, LANES)], edge_x.at[0], edge_send.at[2], edge_recv.at[2], space=right),
        remote(x_hbm.at[0, :, :, pl.ds(0, LANES)], edge_x.at[1], edge_send.at[3], edge_recv.at[3], space=left),
    ]
    for copy in edges:
        copy.start()
    before = jnp.maximum(c - 1, 0)
    nexts = [
        remote(scl_hbm.at[0], next_scl, next_send.at[0], next_recv.at[0], cuts=before),
        remote(x_hbm.at[0], next_x, next_send.at[1], next_recv.at[1], cuts=before),
    ]

    def old_copy():
        return remote(old_out, old_in, next_send.at[2], next_recv.at[2], cuts=before)

    @pl.when(c > 0)
    def _():
        nexts[0].start()

    @pl.when(c > 1)
    def _():
        nexts[1].start()

    @pl.when(member)
    def _():
        @pl.loop(0, c)
        def _(n):
            pl.semaphore_signal(ready.at[me], inc=1, device_id={"cuts": n}, device_id_type=MESH)

    for copy in inputs:
        copy.wait()

    @pl.when(c == 1)
    def _():
        for f in range(2):
            old_out[:, pl.ds(f * cl, cl)] = (scl_in[0, f, :][None] * x_in[0, :, f, :]).astype(jnp.bfloat16)
        old_copy().start()

    table = fric_in[...]
    here = phases(pipe_in[...], table)
    for r in range(REFINE):
        for v in range(nv):
            rates[r, :, pl.ds(v * LANES, LANES)] = jnp.broadcast_to(here[r][v], (scen, LANES))
    head, flow = x_in[0, :, 0, :], x_in[0, :, 1, :]
    fwd, bwd = (head + flow,) * REFINE, (head - flow,) * REFINE
    for _ in range(STEPS):
        fwd, bwd = advance(fwd, bwd, [rates[r] for r in range(REFINE)])
    for f, value in enumerate(coarse(fwd, bwd)):
        own[:, pl.ds(f * cl, cl)] = value

    @pl.when(member)
    def _():
        rearrange(0, chunks)

    def sweep_ends():
        for copy in edges:
            copy.wait()
        lane = lax.broadcasted_iota(jnp.int32, (1, LANES), 1)
        half = lane < HALF

        def ends(own_first, own_last, left_last, right_first):
            return jnp.where(
                half,
                pltpu.roll(jnp.where(half, right_first, own_last), SIDE, 1),
                pltpu.roll(jnp.where(half, own_first, left_last), LANES - SIDE, 1),
            )

        near = phases(
            jnp.concatenate([edge_pipe[0, pl.ds(tall - REFINE, REFINE)], edge_pipe[1, pl.ds(0, REFINE)]], axis=0), table
        )
        end_rates = [
            ends(*(jnp.broadcast_to(v, (8, LANES)) for v in (here[r][0], here[r][-1], near[r][0], near[r][1])))
            for r in range(REFINE)
        ]
        has_right = (s < space - 1).astype(jnp.float32)
        has_left = (s > 0).astype(jnp.float32)
        keep = jnp.where(
            lane < SIDE, 1.0, jnp.where(half, has_right, jnp.where(lane < LANES - SIDE, has_left, 1.0))
        )
        head, flow = (
            keep * ends(x_in[0, :, f, pl.ds(0, LANES)], x_in[0, :, f, pl.ds(cl - LANES, LANES)], edge_x[0, :, f, :], edge_x[1, :, f, :])
            for f in range(2)
        )
        head, flow = head.reshape(-1, 8, LANES), flow.reshape(-1, 8, LANES)
        fwd, bwd = (head + flow,) * REFINE, (head - flow,) * REFINE
        end_rates, keeps = neighbours(end_rates), neighbours([jnp.broadcast_to(keep, (8, LANES))] * REFINE)
        for _ in range(STEPS // REFINE):
            fwd, bwd = advance_phases(fwd, bwd, end_rates, keeps)
        for f, value in enumerate(coarse(fwd, bwd)):
            value = value.reshape(scen, LANES)
            first, final = pl.ds(f * cl, LANES), pl.ds((f + 1) * cl - LANES, LANES)
            own[:, first] = jnp.where(lane < REACH, pltpu.roll(value, SIDE, 1), own[:, first])
            own[:, final] = jnp.where(lane >= LANES - REACH, pltpu.roll(value, LANES - SIDE, 1), own[:, final])

    @pl.when(jnp.logical_not(member))
    def _():
        sweep_ends()

    def start_copy(p, d):
        t = lax.rem(s + d, space)
        return remote(
            start.at[p], xg.at[1, s], start_send.at[p, d], start_recv.at[s], cuts=base + p, space=t
        )

    def dl_copy(n, p):
        return remote(pack.at[p], dl.at[n], dl_send.at[p], dl_recv.at[n], cuts=base + p)

    def res_copy(m, p):
        return remote(res_out.at[m], res_in.at[p], res_send.at[m], res_recv.at[p], cuts=m)

    def last_copy(d):
        return remote(
            last_out, last_in.at[s, me], last_send.at[d], last_recv.at[me, s],
            cuts=last, space=lax.rem(s + d, space),
        )

    def forcing(f):
        return next_scl[f, :][None] * (own[:, pl.ds(f * cl, cl)] - next_x[:, f, :])

    @pl.when(c == 0)
    def _():
        nexts[0].wait_recv()
        old_copy().wait_recv()
        for f in range(2):
            at = pl.ds(f * cl, cl)
            u = next_scl[f, :][None] * own[:, at] - old_in[:, at].astype(jnp.float32)
            for p in range(groups):
                start[p, f] = u[p * share : (p + 1) * share].astype(jnp.bfloat16)

        @pl.loop(0, groups)
        def _(p):
            pl.semaphore_wait(ready.at[p], 1)
            for d in range(space):
                start_copy(p, d).start()

    def send_forcing():
        @pl.when(jnp.logical_and(c > 0, c < last))
        def _():
            for copy in nexts:
                copy.wait_recv()
            for f in range(2):
                u = forcing(f)
                for p in range(groups):
                    pack[p, pl.ds(0, share), pl.ds(f * cl, cl)] = u[p * share : (p + 1) * share]
            for p in range(groups):
                pack[p, pl.ds(0, 2), pl.ds(width, cl)] = next_scl[...]

            @pl.loop(0, groups)
            def _(p):
                @pl.when(base + p > c)
                def _():
                    pl.semaphore_wait(ready.at[p], 1)

                @pl.when(base + p != c)
                def _():
                    dl_copy(c, p).start()

                @pl.when(base + p == c)
                def _():
                    dl[base + p] = pack[p]

    @pl.when(jnp.logical_not(member))
    def _():
        send_forcing()

    def apply_piece(piece, t):
        return lax.dot_general(
            piece, weight[t], (((1,), (0,)), ((), ())), preferred_element_type=jnp.float32
        )

    def apply_half(slot, t, q, columns):
        return lax.dot_general(
            xg[slot, t, q], weight[t, pl.ds(q * cl, cl), columns], (((1,), (0,)), ((), ())),
            preferred_element_type=jnp.float32,
        )

    core = lax.rem(s, 2)

    def peer_of(j):
        return lax.bitwise_xor(s, j if j == 1 else lax.bitwise_xor(j, 1 - core))

    def group_copy(slot, j, f):
        return remote(
            xg.at[slot, s, f], xg.at[slot, s, f], xg_send.at[slot, j, f], xg_recv.at[slot, s, f], space=peer_of(j)
        )

    def group_wait(m, t, f):
        slot = lax.rem(m, 2)

        @pl.when(m > 1)
        def _():
            remote(
                xg.at[slot, t, f], xg.at[slot, t, f], xg_send.at[slot, 0, f], xg_recv.at[slot, t, f], space=t
            ).wait_recv()

        if f == 0:
            @pl.when(m == 1)
            def _():
                remote(xg.at[1, t], xg.at[1, t], start_send.at[0, 0], start_recv.at[t], cuts=0, space=t).wait_recv()

    every = pl.ds(0, width)

    def most_of(m):
        slot = lax.rem(m, 2)

        @pl.when(m == 1)
        def _():
            group_wait(1, s, 0)

        total = apply_half(slot, s, 0, every) + apply_half(slot, s, 1, every)
        for j in range(1, space):
            peer = peer_of(j)
            for f in range(2):
                group_wait(m, peer, f)
                if (j, f) != (space - 1, 1):
                    total += apply_half(slot, peer, f, every)
                else:
                    @pl.when(m != c)
                    def _():
                        dl_copy(m, me).wait_recv()

        return total

    def column_half(m, total, f):
        part = apply_half(lax.rem(m, 2), peer_of(space - 1), 1, pl.ds(f * cl, cl))
        return total[:, f * cl : (f + 1) * cl] + part

    def difference(m, image, f):
        return dl[m, pl.ds(f, 1), pl.ds(width, cl)] * image + dl[
            m, pl.ds(0, share), pl.ds(f * cl, cl)
        ]

    def hand_over(m, image):
        @pl.when(m == c)
        def _():
            res_in[me] = image

        @pl.when(m != c)
        def _():
            res_out[m] = image
            res_copy(m, me).start()

    def sent(m):
        @pl.when(m > 1)
        def _():
            for j in range(1, space):
                for f in range(2):
                    group_copy(lax.rem(m, 2), j, f).wait_send()

    @pl.when(member)
    def _():
        @pl.loop(1, last - 1)
        def _(m):
            total = most_of(m)
            slot = lax.rem(m + 1, 2)
            halves = []
            for f in range(2):
                halves.append(column_half(m, total, f))
                xg[slot, s, f] = difference(m, halves[f], f).astype(jnp.bfloat16)
                for j in reversed(range(1, space)):
                    group_copy(slot, j, f).start()
            hand_over(m, jnp.concatenate(halves, axis=1))

            @pl.when(m == 1)
            def _():
                sweep_ends()
                send_forcing()

            sent(m)

        total = most_of(last - 1)
        halves = []
        for f in range(2):
            halves.append(column_half(last - 1, total, f))
            last_out[:, pl.ds(f * cl, cl)] = difference(last - 1, halves[f], f).astype(jnp.bfloat16)
        image = jnp.concatenate(halves, axis=1)
        for d in range(1, space):
            last_copy(d).start()

        @pl.when(c == last)
        def _():
            last_in[s, groups - 1] = last_out[...]

        @pl.when(c != last)
        def _():
            last_copy(0).start()

        hand_over(last - 1, image)
        sent(last - 1)

    @pl.when(c == 0)
    def _():
        out_ref[...] = own[...]

    @pl.when(c == last)
    def _():
        total = own[...]
        for t in [*range(1, space, 2), *range(0, space, 2)]:
            for p in range(groups):
                @pl.when(jnp.logical_or(base + p != c, t != s))
                def _():
                    remote(
                        last_out, last_in.at[t, p], last_send.at[0], last_recv.at[p, t], cuts=base + p, space=t
                    ).wait_recv()

            piece = jnp.concatenate([last_in[t, p].astype(jnp.float32) for p in range(groups)], axis=0)
            total += apply_piece(piece.astype(jnp.bfloat16), t)
        out_ref[...] = total

    @pl.when(jnp.logical_and(c > 0, c < last))
    def _():
        for p in range(groups):
            @pl.when(base + p != c)
            def _():
                res_copy(c, p).wait_recv()

            at = pl.ds(p * share, share)
            out_ref[at] = res_in[p] + own[at]

    @pl.when(c == 0)
    def _():
        @pl.loop(0, groups)
        def _(p):
            for d in range(space):
                start_copy(p, d).wait_send()

    @pl.when(c > 0)
    def _():
        nexts[0].wait_send()

    @pl.when(c == 1)
    def _():
        old_copy().wait_send()

    @pl.when(c > 1)
    def _():
        nexts[1].wait_send()

    @pl.when(jnp.logical_and(c > 0, c < last))
    def _():
        @pl.loop(0, groups)
        def _(p):
            @pl.when(base + p != c)
            def _():
                dl_copy(c, p).wait_send()

    @pl.when(member)
    def _():
        for d in range(1, space):
            last_copy(d).wait_send()

        @pl.when(c != last)
        def _():
            last_copy(0).wait_send()

        @pl.loop(1, last)
        def _(m):
            @pl.when(m != c)
            def _():
                res_copy(m, me).wait_send()


def solution(mesh):
    cuts, space = mesh.shape["cuts"], mesh.shape["space"]

    def local(start_old, scales, propagator, pipe_of_cell, friction):
        scen, cl = start_old.shape[1], start_old.shape[3]
        cells = propagator.shape[3]
        width = 2 * cl
        groups = math.gcd(GROUPS, math.gcd(cuts, scen))
        share = scen // groups
        pipes = pipe_of_cell.reshape(-1, LANES)
        hbm = pl.BlockSpec(memory_space=pltpu.HBM)
        dma = pltpu.SemaphoreType.DMA
        out = pl.pallas_call(
            functools.partial(kernel, cuts, space, groups),
            out_shape=pltpu.VMEM((scen, width), jnp.float32),
            in_specs=[hbm] * 5,
            out_specs=pl.BlockSpec(memory_space=pltpu.VMEM),
            scratch_shapes=[
                pltpu.VMEM((1, scen, 2, cl), jnp.float32),
                pltpu.VMEM((1, 2, cl), jnp.float32),
                pltpu.VMEM(pipes.shape, jnp.int32),
                pltpu.VMEM((1, LANES), jnp.float32),
                pltpu.VMEM((width, 2, cells), jnp.bfloat16),
                pltpu.VMEM((space, width, width), jnp.bfloat16),
                pltpu.VMEM((REFINE, scen, cl), jnp.float32),
                pltpu.VMEM((2, scen, 2, LANES), jnp.float32),
                pltpu.VMEM((2,) + pipes.shape, jnp.int32),
                pltpu.VMEM((scen, 2, cl), jnp.float32),
                pltpu.VMEM((2, cl), jnp.float32),
                pltpu.VMEM((scen, width), jnp.bfloat16),
                pltpu.VMEM((scen, width), jnp.bfloat16),
                pltpu.VMEM((scen, width), jnp.float32),
                pltpu.VMEM((groups, max(share, 2), width + cl), jnp.float32),
                pltpu.VMEM((cuts, max(share, 2), width + cl), jnp.float32),
                pltpu.VMEM((groups, 2, share, cl), jnp.bfloat16),
                pltpu.VMEM((2, space, 2, share, cl), jnp.bfloat16),
                pltpu.VMEM((share, width), jnp.bfloat16),
                pltpu.VMEM((space, groups, share, width), jnp.bfloat16),
                pltpu.VMEM((cuts, share, width), jnp.float32),
                pltpu.VMEM((groups, share, width), jnp.float32),
                dma((4,)),
                dma((width // ROWS,)),
                pltpu.SemaphoreType.REGULAR((groups,)),
                dma((4,)), dma((4,)),
                dma((3,)), dma((3,)),
                dma((groups,)), dma((cuts,)),
                dma((groups, space)), dma((space,)),
                dma((2, space, 2)), dma((2, space, 2)),
                dma((space,)), dma((groups, space)),
                dma((cuts,)), dma((groups,)),
            ],
            compiler_params=pltpu.CompilerParams(
                collective_id=0, has_side_effects=True, vmem_limit_bytes=60 * 2**20
            ),
        )(start_old, scales, propagator.reshape(width, 2, cells), pipes, friction.reshape(1, -1))
        return out.reshape(1, scen, 2, cl)

    placed = (
        P("cuts", None, None, "space"),
        P("cuts", None, "space"),
        P(None, "space", None, None),
        P("space"),
        P(),
    )
    return jax.shard_map(
        local, mesh=mesh, in_specs=placed, out_specs=P("cuts", None, None, "space"), check_vma=False
    )
```

```python
import functools
import math

import jax
import jax.numpy as jnp
from jax import lax
from jax.experimental import pallas as pl
from jax.experimental.pallas import tpu as pltpu
from jax.sharding import PartitionSpec as P

REFINE = 4
STEPS = 16
LANES = 128
HALF = LANES // 2
ROWS = 128
GROUPS = 4
REACH = STEPS // REFINE
SIDE = LANES // 4
MESH = pl.DeviceIdType.MESH


def phases(pipes, table):
    tall = pipes.shape[0]
    per = LANES // REFINE
    lane = lax.broadcasted_iota(jnp.int32, (tall, LANES), 1)
    row = lax.broadcasted_iota(jnp.int32, (tall, LANES), 0)
    mine = row % REFINE == lane // per
    table = jnp.broadcast_to(table, (tall, LANES))
    out = []
    for r in range(REFINE):
        picked = jnp.take_along_axis(pipes, REFINE * (lane % per) + r, axis=1)
        rate = jnp.where(mine, jnp.take_along_axis(table, picked, axis=1), 0.0)
        out.append([
            jnp.sum(rate[REFINE * v : REFINE * (v + 1)], axis=0, keepdims=True) for v in range(tall // REFINE)
        ])
    return out


def neighbours(values):
    lanes = values[0].shape[-1]

    def rolled(v, by):
        return pltpu.roll(v.reshape(-1, lanes), by, 1).reshape(v.shape)

    return [rolled(v, 1) for v in values] + list(values) + [rolled(v, lanes - 1) for v in values]


def advance_phases(fwd, bwd, rates, keeps):
    fwd, bwd = neighbours(fwd), neighbours(bwd)
    for step in range(REFINE):
        drag = {}
        for i in range(step, 3 * REFINE - step):
            q = 0.5 * (fwd[i] - bwd[i])
            drag[i] = q * jnp.abs(q)
        fwd_new, bwd_new = list(fwd), list(bwd)
        for i in range(step + 1, 3 * REFINE - step - 1):
            fwd_new[i] = keeps[i] * (fwd[i - 1] - rates[i] * drag[i - 1])
            bwd_new[i] = keeps[i] * (bwd[i + 1] + rates[i] * drag[i + 1])
        fwd, bwd = fwd_new, bwd_new
    return tuple(fwd[REFINE : 2 * REFINE]), tuple(bwd[REFINE : 2 * REFINE])


def advance(fwd, bwd, rates):
    lanes = fwd[0].shape[1]
    drag = []
    for r in range(REFINE):
        q = 0.5 * (fwd[r] - bwd[r])
        drag.append(q * jnp.abs(q))
    fwd_new, bwd_new = [], []
    for r in range(REFINE):
        rate = rates[r]
        if r > 0:
            prev_f, prev_d = fwd[r - 1], drag[r - 1]
        else:
            prev_f, prev_d = pltpu.roll(fwd[-1], 1, 1), pltpu.roll(drag[-1], 1, 1)
        if r < REFINE - 1:
            next_b, next_d = bwd[r + 1], drag[r + 1]
        else:
            next_b, next_d = pltpu.roll(bwd[0], lanes - 1, 1), pltpu.roll(drag[0], lanes - 1, 1)
        fwd_new.append(prev_f - rate * prev_d)
        bwd_new.append(next_b + rate * next_d)
    return tuple(fwd_new), tuple(bwd_new)


def coarse(fwd, bwd):
    mean = 0.5 / REFINE
    fwd_sum = fwd[0] + fwd[1] + fwd[2] + fwd[3]
    bwd_sum = bwd[0] + bwd[1] + bwd[2] + bwd[3]
    return mean * (fwd_sum + bwd_sum), mean * (fwd_sum - bwd_sum)


def kernel(
    cuts, space, groups, x_hbm, scl_hbm, prop_hbm, pipe_hbm, fric_hbm, out_ref,
    x_in, scl_in, pipe_in, fric_in, raw, weight, rates, edge_x, edge_pipe, next_x, next_scl, old_out, old_in,
    own, pack, dl, start, xg, last_out, last_in, res_out, res_in,
    in_sem, raw_sem, ready, edge_send, edge_recv, next_send, next_recv, dl_send, dl_recv,
    start_send, start_recv, xg_send, xg_recv, last_send, last_recv, res_send, res_recv,
):
    c = lax.axis_index("cuts")
    s = lax.axis_index("space")
    scen, cl = x_in.shape[1], x_in.shape[3]
    width = 2 * cl
    nv = cl // LANES
    share = scen // groups
    last = cuts - 1
    chunks = raw.shape[0] // ROWS
    tall = pipe_in.shape[0]
    base = cuts - groups
    member = c >= base
    me = jnp.maximum(c - base, 0)

    barrier = pltpu.get_barrier_semaphore()
    for d in range(1, space):
        pl.semaphore_signal(
            barrier, inc=1, device_id={"space": lax.rem(s + d, space)}, device_id_type=MESH
        )

    @pl.when(c + 1 < base)
    def _():
        pl.semaphore_signal(barrier, inc=1, device_id={"cuts": c + 1}, device_id_type=MESH)

    @pl.loop(jnp.maximum(c + 1, base), cuts)
    def _(n):
        pl.semaphore_signal(barrier, inc=1, device_id={"cuts": n}, device_id_type=MESH)

    inputs = [
        pltpu.make_async_copy(pipe_hbm, pipe_in, in_sem.at[0]),
        pltpu.make_async_copy(fric_hbm, fric_in, in_sem.at[1]),
        pltpu.make_async_copy(x_hbm, x_in, in_sem.at[2]),
        pltpu.make_async_copy(scl_hbm, scl_in, in_sem.at[3]),
    ]
    for copy in inputs:
        copy.start()

    def raw_copy(k):
        at = pl.ds(pl.multiple_of(k * ROWS, ROWS), ROWS)
        return pltpu.make_async_copy(prop_hbm.at[at], raw.at[at], raw_sem.at[k])

    @pl.when(member)
    def _():
        for k in range(chunks):
            raw_copy(k).start()

    def remote(src, dst, send, recv, **where):
        return pltpu.make_async_remote_copy(
            src_ref=src, dst_ref=dst, send_sem=send, recv_sem=recv, device_id=where, device_id_type=MESH
        )

    def rearrange(first, stop):
        @pl.loop(first, stop)
        def _(k):
            at = pl.ds(pl.multiple_of(k * ROWS, ROWS), ROWS)
            raw_copy(k).wait()
            fields = pltpu.einshape("rqj->qrj", raw[at])
            for q in range(2):
                for t in range(space):
                    weight[t, pl.ds(q * cl, cl), at] = fields[q][:, t * cl : (t + 1) * cl].T

    pl.semaphore_wait(barrier, space - 1 + jnp.where(member, c, jnp.minimum(c, 1)))

    right, left = lax.rem(s + 1, space), lax.rem(s + space - 1, space)
    edges = [
        remote(pipe_hbm, edge_pipe.at[0], edge_send.at[0], edge_recv.at[0], space=right),
        remote(pipe_hbm, edge_pipe.at[1], edge_send.at[1], edge_recv.at[1], space=left),
        remote(x_hbm.at[0, :, :, pl.ds(cl - LANES, LANES)], edge_x.at[0], edge_send.at[2], edge_recv.at[2], space=right),
        remote(x_hbm.at[0, :, :, pl.ds(0, LANES)], edge_x.at[1], edge_send.at[3], edge_recv.at[3], space=left),
    ]
    for copy in edges:
        copy.start()
    before = jnp.maximum(c - 1, 0)
    nexts = [
        remote(scl_hbm.at[0], next_scl, next_send.at[0], next_recv.at[0], cuts=before),
        remote(x_hbm.at[0], next_x, next_send.at[1], next_recv.at[1], cuts=before),
    ]

    def old_copy():
        return remote(old_out, old_in, next_send.at[2], next_recv.at[2], cuts=before)

    @pl.when(c > 0)
    def _():
        nexts[0].start()

    @pl.when(c > 2)
    def _():
        nexts[1].start()

    @pl.when(member)
    def _():
        @pl.loop(0, c)
        def _(n):
            pl.semaphore_signal(ready.at[me], inc=1, device_id={"cuts": n}, device_id_type=MESH)

    soon = jnp.logical_and(c > 0, c <= 2)
    for copy in inputs:
        copy.wait()

    @pl.when(soon)
    def _():
        for f in range(2):
            old_out[:, pl.ds(f * cl, cl)] = (scl_in[0, f, :][None] * x_in[0, :, f, :]).astype(jnp.bfloat16)
        old_copy().start()

    table = fric_in[...]
    here = phases(pipe_in[...], table)
    for r in range(REFINE):
        for v in range(nv):
            rates[r, :, pl.ds(v * LANES, LANES)] = jnp.broadcast_to(here[r][v], (scen, LANES))
    head, flow = x_in[0, :, 0, :], x_in[0, :, 1, :]
    fwd, bwd = (head + flow,) * REFINE, (head - flow,) * REFINE
    for _ in range(STEPS):
        fwd, bwd = advance(fwd, bwd, [rates[r] for r in range(REFINE)])
    for f, value in enumerate(coarse(fwd, bwd)):
        own[:, pl.ds(f * cl, cl)] = value

    @pl.when(member)
    def _():
        rearrange(0, chunks)

    def sweep_ends():
        for copy in edges:
            copy.wait()
        lane = lax.broadcasted_iota(jnp.int32, (1, LANES), 1)
        half = lane < HALF

        def ends(own_first, own_last, left_last, right_first):
            return jnp.where(
                half,
                pltpu.roll(jnp.where(half, right_first, own_last), SIDE, 1),
                pltpu.roll(jnp.where(half, own_first, left_last), LANES - SIDE, 1),
            )

        near = phases(
            jnp.concatenate([edge_pipe[0, pl.ds(tall - REFINE, REFINE)], edge_pipe[1, pl.ds(0, REFINE)]], axis=0), table
        )
        end_rates = [
            ends(*(jnp.broadcast_to(v, (8, LANES)) for v in (here[r][0], here[r][-1], near[r][0], near[r][1])))
            for r in range(REFINE)
        ]
        has_right = (s < space - 1).astype(jnp.float32)
        has_left = (s > 0).astype(jnp.float32)
        keep = jnp.where(
            lane < SIDE, 1.0, jnp.where(half, has_right, jnp.where(lane < LANES - SIDE, has_left, 1.0))
        )
        head, flow = (
            keep * ends(x_in[0, :, f, pl.ds(0, LANES)], x_in[0, :, f, pl.ds(cl - LANES, LANES)], edge_x[0, :, f, :], edge_x[1, :, f, :])
            for f in range(2)
        )
        head, flow = head.reshape(-1, 8, LANES), flow.reshape(-1, 8, LANES)
        fwd, bwd = (head + flow,) * REFINE, (head - flow,) * REFINE
        end_rates, keeps = neighbours(end_rates), neighbours([jnp.broadcast_to(keep, (8, LANES))] * REFINE)
        for _ in range(STEPS // REFINE):
            fwd, bwd = advance_phases(fwd, bwd, end_rates, keeps)
        for f, value in enumerate(coarse(fwd, bwd)):
            value = value.reshape(scen, LANES)
            first, final = pl.ds(f * cl, LANES), pl.ds((f + 1) * cl - LANES, LANES)
            own[:, first] = jnp.where(lane < REACH, pltpu.roll(value, SIDE, 1), own[:, first])
            own[:, final] = jnp.where(lane >= LANES - REACH, pltpu.roll(value, LANES - SIDE, 1), own[:, final])

    @pl.when(jnp.logical_not(member))
    def _():
        sweep_ends()

    def start_copy(p, d):
        t = lax.rem(s + d, space)
        return remote(
            start.at[p], xg.at[1, s], start_send.at[p, d], start_recv.at[s], cuts=base + p, space=t
        )

    def dl_copy(n, p):
        return remote(pack.at[p], dl.at[n], dl_send.at[p], dl_recv.at[n], cuts=base + p)

    def res_copy(m, p):
        return remote(res_out.at[m], res_in.at[p], res_send.at[m], res_recv.at[p], cuts=m)

    def last_copy(d):
        return remote(
            last_out, last_in.at[s, me], last_send.at[d], last_recv.at[me, s],
            cuts=last, space=lax.rem(s + d, space),
        )

    def forcing_soon(f):
        at = pl.ds(f * cl, cl)
        return next_scl[f, :][None] * own[:, at] - old_in[:, at].astype(jnp.float32)

    def forcing(f):
        return next_scl[f, :][None] * (own[:, pl.ds(f * cl, cl)] - next_x[:, f, :])

    @pl.when(c == 0)
    def _():
        nexts[0].wait_recv()
        old_copy().wait_recv()
        for f in range(2):
            u = forcing_soon(f)
            for p in range(groups):
                start[p, f] = u[p * share : (p + 1) * share].astype(jnp.bfloat16)

        @pl.loop(0, groups)
        def _(p):
            pl.semaphore_wait(ready.at[p], 1)
            for d in range(space):
                start_copy(p, d).start()

    def send_forcing():
        @pl.when(jnp.logical_and(c > 0, c < last))
        def _():
            nexts[0].wait_recv()

            def fill(f, u):
                for p in range(groups):
                    pack[p, pl.ds(0, share), pl.ds(f * cl, cl)] = u[p * share : (p + 1) * share]

            @pl.when(c == 1)
            def _():
                old_copy().wait_recv()
                for f in range(2):
                    fill(f, forcing_soon(f))

            @pl.when(c > 1)
            def _():
                nexts[1].wait_recv()
                for f in range(2):
                    fill(f, forcing(f))

            for p in range(groups):
                pack[p, pl.ds(0, 2), pl.ds(width, cl)] = next_scl[...]

            @pl.loop(0, groups)
            def _(p):
                @pl.when(base + p > c)
                def _():
                    pl.semaphore_wait(ready.at[p], 1)

                @pl.when(base + p != c)
                def _():
                    dl_copy(c, p).start()

                @pl.when(base + p == c)
                def _():
                    dl[base + p] = pack[p]

    @pl.when(jnp.logical_not(member))
    def _():
        send_forcing()

    def apply_piece(piece, t):
        return lax.dot_general(
            piece, weight[t], (((1,), (0,)), ((), ())), preferred_element_type=jnp.float32
        )

    def apply_half(slot, t, q, columns):
        return lax.dot_general(
            xg[slot, t, q], weight[t, pl.ds(q * cl, cl), columns], (((1,), (0,)), ((), ())),
            preferred_element_type=jnp.float32,
        )

    core = lax.rem(s, 2)

    def peer_of(j):
        return lax.bitwise_xor(s, j if j == 1 else lax.bitwise_xor(j, 1 - core))

    def group_copy(slot, j, f):
        return remote(
            xg.at[slot, s, f], xg.at[slot, s, f], xg_send.at[slot, j, f], xg_recv.at[slot, s, f], space=peer_of(j)
        )

    def group_wait(m, t, f):
        slot = lax.rem(m, 2)

        @pl.when(m > 1)
        def _():
            remote(
                xg.at[slot, t, f], xg.at[slot, t, f], xg_send.at[slot, 0, f], xg_recv.at[slot, t, f], space=t
            ).wait_recv()

        if f == 0:
            @pl.when(m == 1)
            def _():
                remote(xg.at[1, t], xg.at[1, t], start_send.at[0, 0], start_recv.at[t], cuts=0, space=t).wait_recv()

    every = pl.ds(0, width)

    def most_of(m):
        slot = lax.rem(m, 2)

        @pl.when(m == 1)
        def _():
            group_wait(1, s, 0)

        total = apply_half(slot, s, 0, every) + apply_half(slot, s, 1, every)
        for j in range(1, space):
            peer = peer_of(j)
            for f in range(2):
                group_wait(m, peer, f)
                if (j, f) != (space - 1, 1):
                    total += apply_half(slot, peer, f, every)
                else:
                    @pl.when(m != c)
                    def _():
                        dl_copy(m, me).wait_recv()

        return total

    def column_half(m, total, f):
        part = apply_half(lax.rem(m, 2), peer_of(space - 1), 1, pl.ds(f * cl, cl))
        return total[:, f * cl : (f + 1) * cl] + part

    def difference(m, image, f):
        return dl[m, pl.ds(f, 1), pl.ds(width, cl)] * image + dl[
            m, pl.ds(0, share), pl.ds(f * cl, cl)
        ]

    def hand_over(m, image):
        @pl.when(m == c)
        def _():
            res_in[me] = image

        @pl.when(m != c)
        def _():
            res_out[m] = image
            res_copy(m, me).start()

    def sent(m):
        @pl.when(m > 1)
        def _():
            for j in range(1, space):
                for f in range(2):
                    group_copy(lax.rem(m, 2), j, f).wait_send()

    @pl.when(member)
    def _():
        @pl.loop(1, last - 1)
        def _(m):
            total = most_of(m)
            slot = lax.rem(m + 1, 2)
            halves = []
            for f in range(2):
                halves.append(column_half(m, total, f))
                xg[slot, s, f] = difference(m, halves[f], f).astype(jnp.bfloat16)
                for j in reversed(range(1, space)):
                    group_copy(slot, j, f).start()
            hand_over(m, jnp.concatenate(halves, axis=1))

            @pl.when(m == 1)
            def _():
                sweep_ends()
                send_forcing()

            sent(m)

        total = most_of(last - 1)
        halves = []
        for f in range(2):
            halves.append(column_half(last - 1, total, f))
            last_out[:, pl.ds(f * cl, cl)] = difference(last - 1, halves[f], f).astype(jnp.bfloat16)
        image = jnp.concatenate(halves, axis=1)
        for d in range(1, space):
            last_copy(d).start()

        @pl.when(c == last)
        def _():
            last_in[s, groups - 1] = last_out[...]

        @pl.when(c != last)
        def _():
            last_copy(0).start()

        hand_over(last - 1, image)
        sent(last - 1)

    @pl.when(c == 0)
    def _():
        out_ref[...] = own[...]

    @pl.when(c == last)
    def _():
        total = own[...]
        for t in [*range(1, space, 2), *range(0, space, 2)]:
            for p in range(groups):
                @pl.when(jnp.logical_or(base + p != c, t != s))
                def _():
                    remote(
                        last_out, last_in.at[t, p], last_send.at[0], last_recv.at[p, t], cuts=base + p, space=t
                    ).wait_recv()

            piece = jnp.concatenate([last_in[t, p].astype(jnp.float32) for p in range(groups)], axis=0)
            total += apply_piece(piece.astype(jnp.bfloat16), t)
        out_ref[...] = total

    @pl.when(jnp.logical_and(c > 0, c < last))
    def _():
        for p in range(groups):
            @pl.when(base + p != c)
            def _():
                res_copy(c, p).wait_recv()

            at = pl.ds(p * share, share)
            out_ref[at] = res_in[p] + own[at]

    @pl.when(c == 0)
    def _():
        @pl.loop(0, groups)
        def _(p):
            for d in range(space):
                start_copy(p, d).wait_send()

    @pl.when(c > 0)
    def _():
        nexts[0].wait_send()

    @pl.when(soon)
    def _():
        old_copy().wait_send()

    @pl.when(c > 2)
    def _():
        nexts[1].wait_send()

    @pl.when(jnp.logical_and(c > 0, c < last))
    def _():
        @pl.loop(0, groups)
        def _(p):
            @pl.when(base + p != c)
            def _():
                dl_copy(c, p).wait_send()

    @pl.when(member)
    def _():
        for d in range(1, space):
            last_copy(d).wait_send()

        @pl.when(c != last)
        def _():
            last_copy(0).wait_send()

        @pl.loop(1, last)
        def _(m):
            @pl.when(m != c)
            def _():
                res_copy(m, me).wait_send()


def solution(mesh):
    cuts, space = mesh.shape["cuts"], mesh.shape["space"]

    def local(start_old, scales, propagator, pipe_of_cell, friction):
        scen, cl = start_old.shape[1], start_old.shape[3]
        cells = propagator.shape[3]
        width = 2 * cl
        groups = math.gcd(GROUPS, math.gcd(cuts, scen))
        share = scen // groups
        pipes = pipe_of_cell.reshape(-1, LANES)
        hbm = pl.BlockSpec(memory_space=pltpu.HBM)
        dma = pltpu.SemaphoreType.DMA
        out = pl.pallas_call(
            functools.partial(kernel, cuts, space, groups),
            out_shape=pltpu.VMEM((scen, width), jnp.float32),
            in_specs=[hbm] * 5,
            out_specs=pl.BlockSpec(memory_space=pltpu.VMEM),
            scratch_shapes=[
                pltpu.VMEM((1, scen, 2, cl), jnp.float32),
                pltpu.VMEM((1, 2, cl), jnp.float32),
                pltpu.VMEM(pipes.shape, jnp.int32),
                pltpu.VMEM((1, LANES), jnp.float32),
                pltpu.VMEM((width, 2, cells), jnp.bfloat16),
                pltpu.VMEM((space, width, width), jnp.bfloat16),
                pltpu.VMEM((REFINE, scen, cl), jnp.float32),
                pltpu.VMEM((2, scen, 2, LANES), jnp.float32),
                pltpu.VMEM((2,) + pipes.shape, jnp.int32),
                pltpu.VMEM((scen, 2, cl), jnp.float32),
                pltpu.VMEM((2, cl), jnp.float32),
                pltpu.VMEM((scen, width), jnp.bfloat16),
                pltpu.VMEM((scen, width), jnp.bfloat16),
                pltpu.VMEM((scen, width), jnp.float32),
                pltpu.VMEM((groups, max(share, 2), width + cl), jnp.float32),
                pltpu.VMEM((cuts, max(share, 2), width + cl), jnp.float32),
                pltpu.VMEM((groups, 2, share, cl), jnp.bfloat16),
                pltpu.VMEM((2, space, 2, share, cl), jnp.bfloat16),
                pltpu.VMEM((share, width), jnp.bfloat16),
                pltpu.VMEM((space, groups, share, width), jnp.bfloat16),
                pltpu.VMEM((cuts, share, width), jnp.float32),
                pltpu.VMEM((groups, share, width), jnp.float32),
                dma((4,)),
                dma((width // ROWS,)),
                pltpu.SemaphoreType.REGULAR((groups,)),
                dma((4,)), dma((4,)),
                dma((3,)), dma((3,)),
                dma((groups,)), dma((cuts,)),
                dma((groups, space)), dma((space,)),
                dma((2, space, 2)), dma((2, space, 2)),
                dma((space,)), dma((groups, space)),
                dma((cuts,)), dma((groups,)),
            ],
            compiler_params=pltpu.CompilerParams(
                collective_id=0, has_side_effects=True, vmem_limit_bytes=60 * 2**20
            ),
        )(start_old, scales, propagator.reshape(width, 2, cells), pipes, friction.reshape(1, -1))
        return out.reshape(1, scen, 2, cl)

    placed = (
        P("cuts", None, None, "space"),
        P("cuts", None, "space"),
        P(None, "space", None, None),
        P("space"),
        P(),
    )
    return jax.shard_map(
        local, mesh=mesh, in_specs=placed, out_specs=P("cuts", None, None, "space"), check_vma=False
    )
```

```python
import functools
import math

import jax
import jax.numpy as jnp
from jax import lax
from jax.experimental import pallas as pl
from jax.experimental.pallas import tpu as pltpu
from jax.sharding import PartitionSpec as P

REFINE = 4
STEPS = 16
LANES = 128
HALF = LANES // 2
ROWS = 256
GROUPS = 4
REACH = STEPS // REFINE
SIDE = LANES // 4
MESH = pl.DeviceIdType.MESH


def phases(pipes, table):
    tall = pipes.shape[0]
    per = LANES // REFINE
    lane = lax.broadcasted_iota(jnp.int32, (tall, LANES), 1)
    row = lax.broadcasted_iota(jnp.int32, (tall, LANES), 0)
    mine = row % REFINE == lane // per
    table = jnp.broadcast_to(table, (tall, LANES))
    out = []
    for r in range(REFINE):
        picked = jnp.take_along_axis(pipes, REFINE * (lane % per) + r, axis=1)
        rate = jnp.where(mine, jnp.take_along_axis(table, picked, axis=1), 0.0)
        out.append([
            jnp.sum(rate[REFINE * v : REFINE * (v + 1)], axis=0, keepdims=True) for v in range(tall // REFINE)
        ])
    return out


def neighbours(values):
    lanes = values[0].shape[-1]

    def rolled(v, by):
        return pltpu.roll(v.reshape(-1, lanes), by, 1).reshape(v.shape)

    return [rolled(v, 1) for v in values] + list(values) + [rolled(v, lanes - 1) for v in values]


def advance_phases(fwd, bwd, rates, keeps):
    fwd, bwd = neighbours(fwd), neighbours(bwd)
    for step in range(REFINE):
        drag = {}
        for i in range(step, 3 * REFINE - step):
            q = 0.5 * (fwd[i] - bwd[i])
            drag[i] = q * jnp.abs(q)
        fwd_new, bwd_new = list(fwd), list(bwd)
        for i in range(step + 1, 3 * REFINE - step - 1):
            fwd_new[i] = keeps[i] * (fwd[i - 1] - rates[i] * drag[i - 1])
            bwd_new[i] = keeps[i] * (bwd[i + 1] + rates[i] * drag[i + 1])
        fwd, bwd = fwd_new, bwd_new
    return tuple(fwd[REFINE : 2 * REFINE]), tuple(bwd[REFINE : 2 * REFINE])


def advance(fwd, bwd, rates):
    lanes = fwd[0].shape[1]
    drag = []
    for r in range(REFINE):
        q = 0.5 * (fwd[r] - bwd[r])
        drag.append(q * jnp.abs(q))
    fwd_new, bwd_new = [], []
    for r in range(REFINE):
        rate = rates[r]
        if r > 0:
            prev_f, prev_d = fwd[r - 1], drag[r - 1]
        else:
            prev_f, prev_d = pltpu.roll(fwd[-1], 1, 1), pltpu.roll(drag[-1], 1, 1)
        if r < REFINE - 1:
            next_b, next_d = bwd[r + 1], drag[r + 1]
        else:
            next_b, next_d = pltpu.roll(bwd[0], lanes - 1, 1), pltpu.roll(drag[0], lanes - 1, 1)
        fwd_new.append(prev_f - rate * prev_d)
        bwd_new.append(next_b + rate * next_d)
    return tuple(fwd_new), tuple(bwd_new)


def coarse(fwd, bwd):
    mean = 0.5 / REFINE
    fwd_sum = fwd[0] + fwd[1] + fwd[2] + fwd[3]
    bwd_sum = bwd[0] + bwd[1] + bwd[2] + bwd[3]
    return mean * (fwd_sum + bwd_sum), mean * (fwd_sum - bwd_sum)


def kernel(
    cuts, space, groups, x_hbm, scl_hbm, prop_hbm, pipe_hbm, fric_hbm, out_ref,
    x_in, scl_in, pipe_in, fric_in, raw, weight, rates, edge_x, edge_pipe, next_x, next_scl, old_out, old_in,
    own, pack, dl, start, xg, last_out, last_in, res_out, res_in,
    in_sem, raw_sem, ready, edge_send, edge_recv, next_send, next_recv, dl_send, dl_recv,
    start_send, start_recv, xg_send, xg_recv, last_send, last_recv, res_send, res_recv,
):
    c = lax.axis_index("cuts")
    s = lax.axis_index("space")
    scen, cl = x_in.shape[1], x_in.shape[3]
    width = 2 * cl
    nv = cl // LANES
    share = scen // groups
    last = cuts - 1
    chunks = raw.shape[0] // ROWS
    tall = pipe_in.shape[0]
    base = cuts - groups
    member = c >= base
    me = jnp.maximum(c - base, 0)

    barrier = pltpu.get_barrier_semaphore()
    for d in range(1, space):
        pl.semaphore_signal(
            barrier, inc=1, device_id={"space": lax.rem(s + d, space)}, device_id_type=MESH
        )

    @pl.when(c + 1 < base)
    def _():
        pl.semaphore_signal(barrier, inc=1, device_id={"cuts": c + 1}, device_id_type=MESH)

    @pl.loop(jnp.maximum(c + 1, base), cuts)
    def _(n):
        pl.semaphore_signal(barrier, inc=1, device_id={"cuts": n}, device_id_type=MESH)

    inputs = [
        pltpu.make_async_copy(pipe_hbm, pipe_in, in_sem.at[0]),
        pltpu.make_async_copy(fric_hbm, fric_in, in_sem.at[1]),
        pltpu.make_async_copy(x_hbm, x_in, in_sem.at[2]),
        pltpu.make_async_copy(scl_hbm, scl_in, in_sem.at[3]),
    ]
    for copy in inputs:
        copy.start()

    def raw_copy(k):
        at = pl.ds(pl.multiple_of(k * ROWS, ROWS), ROWS)
        return pltpu.make_async_copy(prop_hbm.at[at], raw.at[at], raw_sem.at[k])

    @pl.when(member)
    def _():
        for k in range(chunks):
            raw_copy(k).start()

    def remote(src, dst, send, recv, **where):
        return pltpu.make_async_remote_copy(
            src_ref=src, dst_ref=dst, send_sem=send, recv_sem=recv, device_id=where, device_id_type=MESH
        )

    def rearrange(first, stop):
        @pl.loop(first, stop)
        def _(k):
            at = pl.ds(pl.multiple_of(k * ROWS, ROWS), ROWS)
            raw_copy(k).wait()
            fields = pltpu.einshape("rqj->qrj", raw[at])
            for q in range(2):
                for t in range(space):
                    weight[t, pl.ds(q * cl, cl), at] = fields[q][:, t * cl : (t + 1) * cl].T

    pl.semaphore_wait(barrier, space - 1 + jnp.where(member, c, jnp.minimum(c, 1)))

    right, left = lax.rem(s + 1, space), lax.rem(s + space - 1, space)
    edges = [
        remote(pipe_hbm, edge_pipe.at[0], edge_send.at[0], edge_recv.at[0], space=right),
        remote(pipe_hbm, edge_pipe.at[1], edge_send.at[1], edge_recv.at[1], space=left),
        remote(x_hbm.at[0, :, :, pl.ds(cl - LANES, LANES)], edge_x.at[0], edge_send.at[2], edge_recv.at[2], space=right),
        remote(x_hbm.at[0, :, :, pl.ds(0, LANES)], edge_x.at[1], edge_send.at[3], edge_recv.at[3], space=left),
    ]
    for copy in edges:
        copy.start()
    before = jnp.maximum(c - 1, 0)
    nexts = [
        remote(scl_hbm.at[0], next_scl, next_send.at[0], next_recv.at[0], cuts=before),
        remote(x_hbm.at[0], next_x, next_send.at[1], next_recv.at[1], cuts=before),
    ]

    def old_copy():
        return remote(old_out, old_in, next_send.at[2], next_recv.at[2], cuts=before)

    @pl.when(c > 0)
    def _():
        nexts[0].start()

    @pl.when(c > 2)
    def _():
        nexts[1].start()

    @pl.when(member)
    def _():
        @pl.loop(0, c)
        def _(n):
            pl.semaphore_signal(ready.at[me], inc=1, device_id={"cuts": n}, device_id_type=MESH)

    soon = jnp.logical_and(c > 0, c <= 2)
    for copy in inputs:
        copy.wait()

    @pl.when(soon)
    def _():
        for f in range(2):
            old_out[:, pl.ds(f * cl, cl)] = (scl_in[0, f, :][None] * x_in[0, :, f, :]).astype(jnp.bfloat16)
        old_copy().start()

    table = fric_in[...]
    here = phases(pipe_in[...], table)
    for r in range(REFINE):
        for v in range(nv):
            rates[r, :, pl.ds(v * LANES, LANES)] = jnp.broadcast_to(here[r][v], (scen, LANES))
    head, flow = x_in[0, :, 0, :], x_in[0, :, 1, :]
    fwd, bwd = (head + flow,) * REFINE, (head - flow,) * REFINE
    for _ in range(STEPS):
        fwd, bwd = advance(fwd, bwd, [rates[r] for r in range(REFINE)])
    for f, value in enumerate(coarse(fwd, bwd)):
        own[:, pl.ds(f * cl, cl)] = value

    @pl.when(member)
    def _():
        rearrange(0, chunks)

    def sweep_ends():
        for copy in edges:
            copy.wait()
        lane = lax.broadcasted_iota(jnp.int32, (1, LANES), 1)
        half = lane < HALF

        def ends(own_first, own_last, left_last, right_first):
            return jnp.where(
                half,
                pltpu.roll(jnp.where(half, right_first, own_last), SIDE, 1),
                pltpu.roll(jnp.where(half, own_first, left_last), LANES - SIDE, 1),
            )

        near = phases(
            jnp.concatenate([edge_pipe[0, pl.ds(tall - REFINE, REFINE)], edge_pipe[1, pl.ds(0, REFINE)]], axis=0), table
        )
        end_rates = [
            ends(*(jnp.broadcast_to(v, (8, LANES)) for v in (here[r][0], here[r][-1], near[r][0], near[r][1])))
            for r in range(REFINE)
        ]
        has_right = (s < space - 1).astype(jnp.float32)
        has_left = (s > 0).astype(jnp.float32)
        keep = jnp.where(
            lane < SIDE, 1.0, jnp.where(half, has_right, jnp.where(lane < LANES - SIDE, has_left, 1.0))
        )
        head, flow = (
            keep * ends(x_in[0, :, f, pl.ds(0, LANES)], x_in[0, :, f, pl.ds(cl - LANES, LANES)], edge_x[0, :, f, :], edge_x[1, :, f, :])
            for f in range(2)
        )
        head, flow = head.reshape(-1, 8, LANES), flow.reshape(-1, 8, LANES)
        fwd, bwd = (head + flow,) * REFINE, (head - flow,) * REFINE
        end_rates, keeps = neighbours(end_rates), neighbours([jnp.broadcast_to(keep, (8, LANES))] * REFINE)
        for _ in range(STEPS // REFINE):
            fwd, bwd = advance_phases(fwd, bwd, end_rates, keeps)
        for f, value in enumerate(coarse(fwd, bwd)):
            value = value.reshape(scen, LANES)
            first, final = pl.ds(f * cl, LANES), pl.ds((f + 1) * cl - LANES, LANES)
            own[:, first] = jnp.where(lane < REACH, pltpu.roll(value, SIDE, 1), own[:, first])
            own[:, final] = jnp.where(lane >= LANES - REACH, pltpu.roll(value, LANES - SIDE, 1), own[:, final])

    @pl.when(jnp.logical_not(member))
    def _():
        sweep_ends()

    def start_copy(p, d):
        t = lax.rem(s + d, space)
        return remote(
            start.at[p], xg.at[1, s], start_send.at[p, d], start_recv.at[s], cuts=base + p, space=t
        )

    def dl_copy(n, p):
        return remote(pack.at[p], dl.at[n], dl_send.at[p], dl_recv.at[n], cuts=base + p)

    def res_copy(m, p):
        return remote(res_out.at[m], res_in.at[p], res_send.at[m], res_recv.at[p], cuts=m)

    def last_copy(d):
        return remote(
            last_out, last_in.at[s, me], last_send.at[d], last_recv.at[me, s],
            cuts=last, space=lax.rem(s + d, space),
        )

    def forcing_soon(f):
        at = pl.ds(f * cl, cl)
        return next_scl[f, :][None] * own[:, at] - old_in[:, at].astype(jnp.float32)

    def forcing(f):
        return next_scl[f, :][None] * (own[:, pl.ds(f * cl, cl)] - next_x[:, f, :])

    @pl.when(c == 0)
    def _():
        nexts[0].wait_recv()
        old_copy().wait_recv()
        for f in range(2):
            u = forcing_soon(f)
            for p in range(groups):
                start[p, f] = u[p * share : (p + 1) * share].astype(jnp.bfloat16)

        @pl.loop(0, groups)
        def _(p):
            pl.semaphore_wait(ready.at[p], 1)
            for d in range(space):
                start_copy(p, d).start()

    def send_forcing():
        @pl.when(jnp.logical_and(c > 0, c < last))
        def _():
            nexts[0].wait_recv()

            def fill(f, u):
                for p in range(groups):
                    pack[p, pl.ds(0, share), pl.ds(f * cl, cl)] = u[p * share : (p + 1) * share]

            @pl.when(c == 1)
            def _():
                old_copy().wait_recv()
                for f in range(2):
                    fill(f, forcing_soon(f))

            @pl.when(c > 1)
            def _():
                nexts[1].wait_recv()
                for f in range(2):
                    fill(f, forcing(f))

            for p in range(groups):
                pack[p, pl.ds(0, 2), pl.ds(width, cl)] = next_scl[...]

            @pl.loop(0, groups)
            def _(p):
                @pl.when(base + p > c)
                def _():
                    pl.semaphore_wait(ready.at[p], 1)

                @pl.when(base + p != c)
                def _():
                    dl_copy(c, p).start()

                @pl.when(base + p == c)
                def _():
                    dl[base + p] = pack[p]

    @pl.when(jnp.logical_not(member))
    def _():
        send_forcing()

    def apply_piece(piece, t):
        return lax.dot_general(
            piece, weight[t], (((1,), (0,)), ((), ())), preferred_element_type=jnp.float32
        )

    def apply_half(slot, t, q, columns):
        return lax.dot_general(
            xg[slot, t, q], weight[t, pl.ds(q * cl, cl), columns], (((1,), (0,)), ((), ())),
            preferred_element_type=jnp.float32,
        )

    core = lax.rem(s, 2)

    def peer_of(j):
        return lax.bitwise_xor(s, j if j == 1 else lax.bitwise_xor(j, 1 - core))

    def group_copy(slot, j, f):
        return remote(
            xg.at[slot, s, f], xg.at[slot, s, f], xg_send.at[slot, j, f], xg_recv.at[slot, s, f], space=peer_of(j)
        )

    def group_wait(m, t, f):
        slot = lax.rem(m, 2)

        @pl.when(m > 1)
        def _():
            remote(
                xg.at[slot, t, f], xg.at[slot, t, f], xg_send.at[slot, 0, f], xg_recv.at[slot, t, f], space=t
            ).wait_recv()

        if f == 0:
            @pl.when(m == 1)
            def _():
                remote(xg.at[1, t], xg.at[1, t], start_send.at[0, 0], start_recv.at[t], cuts=0, space=t).wait_recv()

    every = pl.ds(0, width)

    def most_of(m):
        slot = lax.rem(m, 2)

        @pl.when(m == 1)
        def _():
            group_wait(1, s, 0)

        total = apply_half(slot, s, 0, every) + apply_half(slot, s, 1, every)
        for j in range(1, space):
            peer = peer_of(j)
            for f in range(2):
                group_wait(m, peer, f)
                if (j, f) != (space - 1, 1):
                    total += apply_half(slot, peer, f, every)
                else:
                    @pl.when(m != c)
                    def _():
                        dl_copy(m, me).wait_recv()

        return total

    def column_half(m, total, f):
        part = apply_half(lax.rem(m, 2), peer_of(space - 1), 1, pl.ds(f * cl, cl))
        return total[:, f * cl : (f + 1) * cl] + part

    def difference(m, image, f):
        return dl[m, pl.ds(f, 1), pl.ds(width, cl)] * image + dl[
            m, pl.ds(0, share), pl.ds(f * cl, cl)
        ]

    def hand_over(m, image):
        @pl.when(m == c)
        def _():
            res_in[me] = image

        @pl.when(m != c)
        def _():
            res_out[m] = image
            res_copy(m, me).start()

    def sent(m):
        @pl.when(m > 1)
        def _():
            for j in range(1, space):
                for f in range(2):
                    group_copy(lax.rem(m, 2), j, f).wait_send()

    @pl.when(member)
    def _():
        @pl.loop(1, last - 1)
        def _(m):
            total = most_of(m)
            slot = lax.rem(m + 1, 2)
            halves = []
            for f in range(2):
                halves.append(column_half(m, total, f))
                xg[slot, s, f] = difference(m, halves[f], f).astype(jnp.bfloat16)
                for j in reversed(range(1, space)):
                    group_copy(slot, j, f).start()
            hand_over(m, jnp.concatenate(halves, axis=1))

            @pl.when(m == 1)
            def _():
                sweep_ends()
                send_forcing()

            sent(m)

        total = most_of(last - 1)
        halves = []
        for f in range(2):
            halves.append(column_half(last - 1, total, f))
            last_out[:, pl.ds(f * cl, cl)] = difference(last - 1, halves[f], f).astype(jnp.bfloat16)
        image = jnp.concatenate(halves, axis=1)
        for d in range(1, space):
            last_copy(d).start()

        @pl.when(c == last)
        def _():
            last_in[s, groups - 1] = last_out[...]

        @pl.when(c != last)
        def _():
            last_copy(0).start()

        hand_over(last - 1, image)
        sent(last - 1)

    @pl.when(c == 0)
    def _():
        out_ref[...] = own[...]

    @pl.when(c == last)
    def _():
        total = own[...]
        for t in [*range(1, space, 2), *range(0, space, 2)]:
            for p in range(groups):
                @pl.when(jnp.logical_or(base + p != c, t != s))
                def _():
                    remote(
                        last_out, last_in.at[t, p], last_send.at[0], last_recv.at[p, t], cuts=base + p, space=t
                    ).wait_recv()

            piece = jnp.concatenate([last_in[t, p].astype(jnp.float32) for p in range(groups)], axis=0)
            total += apply_piece(piece.astype(jnp.bfloat16), t)
        out_ref[...] = total

    @pl.when(jnp.logical_and(c > 0, c < last))
    def _():
        for p in range(groups):
            @pl.when(base + p != c)
            def _():
                res_copy(c, p).wait_recv()

            at = pl.ds(p * share, share)
            out_ref[at] = res_in[p] + own[at]

    @pl.when(c == 0)
    def _():
        @pl.loop(0, groups)
        def _(p):
            for d in range(space):
                start_copy(p, d).wait_send()

    @pl.when(c > 0)
    def _():
        nexts[0].wait_send()

    @pl.when(soon)
    def _():
        old_copy().wait_send()

    @pl.when(c > 2)
    def _():
        nexts[1].wait_send()

    @pl.when(jnp.logical_and(c > 0, c < last))
    def _():
        @pl.loop(0, groups)
        def _(p):
            @pl.when(base + p != c)
            def _():
                dl_copy(c, p).wait_send()

    @pl.when(member)
    def _():
        for d in range(1, space):
            last_copy(d).wait_send()

        @pl.when(c != last)
        def _():
            last_copy(0).wait_send()

        @pl.loop(1, last)
        def _(m):
            @pl.when(m != c)
            def _():
                res_copy(m, me).wait_send()


def solution(mesh):
    cuts, space = mesh.shape["cuts"], mesh.shape["space"]

    def local(start_old, scales, propagator, pipe_of_cell, friction):
        scen, cl = start_old.shape[1], start_old.shape[3]
        cells = propagator.shape[3]
        width = 2 * cl
        groups = math.gcd(GROUPS, math.gcd(cuts, scen))
        share = scen // groups
        pipes = pipe_of_cell.reshape(-1, LANES)
        hbm = pl.BlockSpec(memory_space=pltpu.HBM)
        dma = pltpu.SemaphoreType.DMA
        out = pl.pallas_call(
            functools.partial(kernel, cuts, space, groups),
            out_shape=pltpu.VMEM((scen, width), jnp.float32),
            in_specs=[hbm] * 5,
            out_specs=pl.BlockSpec(memory_space=pltpu.VMEM),
            scratch_shapes=[
                pltpu.VMEM((1, scen, 2, cl), jnp.float32),
                pltpu.VMEM((1, 2, cl), jnp.float32),
                pltpu.VMEM(pipes.shape, jnp.int32),
                pltpu.VMEM((1, LANES), jnp.float32),
                pltpu.VMEM((width, 2, cells), jnp.bfloat16),
                pltpu.VMEM((space, width, width), jnp.bfloat16),
                pltpu.VMEM((REFINE, scen, cl), jnp.float32),
                pltpu.VMEM((2, scen, 2, LANES), jnp.float32),
                pltpu.VMEM((2,) + pipes.shape, jnp.int32),
                pltpu.VMEM((scen, 2, cl), jnp.float32),
                pltpu.VMEM((2, cl), jnp.float32),
                pltpu.VMEM((scen, width), jnp.bfloat16),
                pltpu.VMEM((scen, width), jnp.bfloat16),
                pltpu.VMEM((scen, width), jnp.float32),
                pltpu.VMEM((groups, max(share, 2), width + cl), jnp.float32),
                pltpu.VMEM((cuts, max(share, 2), width + cl), jnp.float32),
                pltpu.VMEM((groups, 2, share, cl), jnp.bfloat16),
                pltpu.VMEM((2, space, 2, share, cl), jnp.bfloat16),
                pltpu.VMEM((share, width), jnp.bfloat16),
                pltpu.VMEM((space, groups, share, width), jnp.bfloat16),
                pltpu.VMEM((cuts, share, width), jnp.float32),
                pltpu.VMEM((groups, share, width), jnp.float32),
                dma((4,)),
                dma((width // ROWS,)),
                pltpu.SemaphoreType.REGULAR((groups,)),
                dma((4,)), dma((4,)),
                dma((3,)), dma((3,)),
                dma((groups,)), dma((cuts,)),
                dma((groups, space)), dma((space,)),
                dma((2, space, 2)), dma((2, space, 2)),
                dma((space,)), dma((groups, space)),
                dma((cuts,)), dma((groups,)),
            ],
            compiler_params=pltpu.CompilerParams(
                collective_id=0, has_side_effects=True, vmem_limit_bytes=60 * 2**20
            ),
        )(start_old, scales, propagator.reshape(width, 2, cells), pipes, friction.reshape(1, -1))
        return out.reshape(1, scen, 2, cl)

    placed = (
        P("cuts", None, None, "space"),
        P("cuts", None, "space"),
        P(None, "space", None, None),
        P("space"),
        P(),
    )
    return jax.shard_map(
        local, mesh=mesh, in_specs=placed, out_specs=P("cuts", None, None, "space"), check_vma=False
    )
```
